512 devices in a mesh: box: 128 (over z, y, core), level: 4 (over x).
Axes of the slice: x: 4, y: 4, z: 16, core: 2. Of those that a mesh axis runs over, the one named last changes fastest.
Arguments:
- rhs_field: float32 [4, 2048, 128], P(None, 'box'), may hold values from -6 to 6
- self_coef: float32 [2048, 128], P('box'), may hold values from 2 to 4
- expand: bfloat16 [2048, 256, 128], P('box'), may hold values from -0.5 to 0.5
- near_ops: bfloat16 [26, 128, 128], replicated, may hold values from -0.109375 to 0.109375
- class_ops: bfloat16 [128, 256, 256], P('box', 'level'), may hold values from -0.046875 to 0.046875
- near_src: int32 [2048, 26], P('box'), may hold values from 0 to 47
- send_rows: int32 [128, 128, 2], P('box'), may hold values from 0 to 15
- list_slot: int32 [2048, 64], P('box'), may hold values from 0 to 255
- list_class: int32 [2048, 64], P('box'), may hold values from 0 to 127, all different within a row
Outputs:
- solution: float32 [4, 2048, 128], P(None, 'box')
The draws below stay inside these ranges and needn't reach their ends.
Inputs may be any that keep to these rules, and one draw needn't show every extreme that they name: `near_src`: the near-field neighbours of a box lie among the boxes of the index of box before it, its own and the one after it, counted in that order. `send_rows`: each entry is a box of the sending index. `list_slot`: entry q * 2 + j names the j-th row sent by index q of box. `list_class`: the classes of one box's list are distinct.
All inputs are finite; a program needn't handle non-finite values.
Results may differ from the reference program's by a relative error of at most 0.004.
Values may be sent and summed in bfloat16 or wider, within the bound.
A program may use at most 64 MiB of HBM per device.

```python
import jax
import jax.numpy as jnp
from jax import lax

P_SIZE = 256
PAN = 128
RHS = 4
BOX_DEV = 16
CAP = 2
NNEAR = 26
NBOX = 2048
NCLASS = 128
LIST = 64
N_BOX = 128


def plant(entries, rng, least, top_value):
    index_at = [jax.random.randint(jax.random.fold_in(rng, axis), (), 0, length) for axis, length in enumerate(entries.shape)]
    main_axis = entries.shape.index(max(entries.shape))
    next_to = index_at[:main_axis] + [(index_at[main_axis] + 1) % entries.shape[main_axis]] + index_at[main_axis + 1:]
    return entries.at[tuple(index_at)].set(least).at[tuple(next_to)].set(top_value)


def steps_of(key, extent, pieces, smallest, largest):
    factor_of = 1.0
    for position, shards_of in pieces:
        draws = jax.random.uniform(jax.random.fold_in(jax.random.fold_in(key, 6), position), (shards_of,), jnp.float32, smallest / len(pieces), largest / len(pieces))
        factor_of = factor_of * jnp.repeat(jnp.exp(draws), extent[position] // shards_of).reshape((-1,) + (1,) * (len(extent) - 1 - position))
    return factor_of


def choose_distinct(own_key, rows, amount, top, lift):
    order = jax.random.permutation(jax.random.fold_in(own_key, 1), amount)
    pull = order
    for power in range(3):
        pull = pull * pull // amount
    pull = pull * lift // amount
    tickets = jax.random.randint(jax.random.fold_in(own_key, 2), (rows, amount), 0, 4096) + pull
    fixed_rows = jax.random.permutation(jax.random.fold_in(own_key, 3), rows)[jnp.arange(amount) % rows]
    tickets = jnp.where(jnp.arange(rows)[:, None] == fixed_rows[None, :], 1 << 14, tickets)
    merit = tickets * amount + jnp.arange(amount)
    return lax.top_k(merit.astype(jnp.int32), top)[1].astype(jnp.int32)


def gaussian(own_key, extent, width, limit, shards=(), kind=jnp.bfloat16):
    drawn = width * jax.random.normal(own_key, extent, jnp.float32)
    if shards:
        drawn = drawn * steps_of(own_key, extent, shards, -0.22, 0.18)
    return jnp.clip(drawn, -limit, limit).astype(kind)


def setup_inputs(seed: int = 0) -> dict:
    streams_of = jax.random.split(jax.random.key(seed), 10)
    rhs_field = gaussian(streams_of[0], (RHS, NBOX, PAN), 1.0, 6.0, ((1, 128),), jnp.float32)
    self_coef = jnp.clip(2.0 + 2.0 * jax.random.uniform(streams_of[1], (NBOX, PAN), jnp.float32) ** steps_of(streams_of[1], (NBOX, PAN), ((0, 128),), -0.2, 0.2), 2.0, 4.0)
    expand = gaussian(streams_of[2], (NBOX, P_SIZE, PAN), PAN ** -0.5, 0.5, ((0, 128),))
    near_ops = gaussian(streams_of[3], (NNEAR, PAN, PAN), (PAN * NNEAR) ** -0.5, 0.109375)
    class_ops = gaussian(streams_of[4], (NCLASS, P_SIZE, P_SIZE), (P_SIZE * LIST) ** -0.5, 0.046875, ((0, 128), (1, 4)))
    near_src = plant(jax.random.randint(streams_of[5], (NBOX, NNEAR), 0, 3 * BOX_DEV), jax.random.fold_in(streams_of[5], 1), 0, (3 * BOX_DEV) - 1).astype(jnp.int32)
    send_rows = plant(jax.random.randint(streams_of[6], (N_BOX, N_BOX, CAP), 0, BOX_DEV), jax.random.fold_in(streams_of[6], 1), 0, BOX_DEV - 1).astype(jnp.int32)
    list_slot = plant(jax.random.randint(streams_of[7], (NBOX, LIST), 0, N_BOX * CAP), jax.random.fold_in(streams_of[7], 1), 0, (N_BOX * CAP) - 1).astype(jnp.int32)
    list_class = choose_distinct(streams_of[8], NBOX, NCLASS, LIST, 0)
    return {"rhs_field": rhs_field, "self_coef": self_coef, "expand": expand, "near_ops": near_ops, "class_ops": class_ops, "near_src": near_src, "send_rows": send_rows, "list_slot": list_slot, "list_class": list_class}


def build_table(send_rows, list_slot, list_class):
    owner = jnp.arange(NBOX, dtype=jnp.int32) // BOX_DEV
    sender = (list_slot // CAP).astype(jnp.int32)
    place = (list_slot % CAP).astype(jnp.int32)
    global_src = sender * BOX_DEV + send_rows[sender, owner[:, None], place]
    table = jnp.full((NBOX, NCLASS), -1, jnp.int32)
    targets = jnp.broadcast_to(jnp.arange(NBOX, dtype=jnp.int32)[:, None], list_class.shape)
    return table.at[targets, list_class].set(global_src.astype(jnp.int32))

def apply_matrix(field, self_coef, expand, near_ops, class_ops, near_src, table):
    field_half = field.astype(jnp.bfloat16)
    expand_wide = expand.astype(jnp.float32)
    multipoles = jnp.einsum('tpk,rtk->trp', expand_wide, field_half.astype(jnp.float32)).astype(jnp.bfloat16)

    def add_class(number, totals):
        picked = table[:, number]
        sources = jnp.where((picked >= 0)[:, None, None], multipoles[jnp.maximum(picked, 0)], jnp.zeros((), jnp.bfloat16))
        return totals + jnp.einsum('qp,trp->trq', class_ops[number].astype(jnp.float32), sources.astype(jnp.float32))
    local_full = lax.fori_loop(0, NCLASS, add_class, jnp.zeros((NBOX, RHS, P_SIZE), jnp.float32))
    local_half = local_full.astype(jnp.bfloat16)
    far_part = jnp.einsum('tpk,trp->rtk', expand_wide, local_half.astype(jnp.float32))
    owner_start = jnp.arange(NBOX, dtype=jnp.int32) // BOX_DEV * BOX_DEV - BOX_DEV
    near_global = owner_start[:, None] + near_src
    valid = (near_global >= 0) & (near_global < NBOX)
    safe = jnp.clip(near_global, 0, NBOX - 1).astype(jnp.int32)

    def add_near(number, totals):
        chosen = field_half[:, safe[:, number]]
        chosen = jnp.where(valid[:, number][None, :, None], chosen, jnp.zeros((), jnp.bfloat16))
        return totals + jnp.einsum('ij,rtj->rti', near_ops[number].astype(jnp.float32), chosen.astype(jnp.float32))
    near_part = lax.fori_loop(0, NNEAR, add_near, jnp.zeros((RHS, NBOX, PAN), jnp.float32))
    return self_coef[None] * field + near_part + far_part

def inner(first, second):
    return lax.optimization_barrier(jnp.sum(first * second, axis=(1, 2)))

def spread(values, field):
    return values[:, None, None] * field

def reference(rhs_field, self_coef, expand, near_ops, class_ops, near_src, send_rows, list_slot, list_class):
    table = build_table(send_rows, list_slot, list_class)
    beta = jnp.sqrt(inner(rhs_field, rhs_field))
    first = rhs_field / beta[:, None, None]
    image = apply_matrix(first, self_coef, expand, near_ops, class_ops, near_src, table)
    h_one_one = inner(first, image)
    image = image - spread(h_one_one, first)
    h_two_one = jnp.sqrt(inner(image, image))
    second = image / h_two_one[:, None, None]
    image = apply_matrix(second, self_coef, expand, near_ops, class_ops, near_src, table)
    h_one_two = inner(first, image)
    h_two_two = inner(second, image)
    image = image - spread(h_one_two, first) - spread(h_two_two, second)
    h_three_two = jnp.sqrt(inner(image, image))
    gram_aa = h_one_one * h_one_one + h_two_one * h_two_one
    gram_ab = h_one_one * h_one_two + h_two_one * h_two_two
    gram_bb = h_one_two * h_one_two + h_two_two * h_two_two + h_three_two * h_three_two
    right_a = beta * h_one_one
    right_b = beta * h_one_two
    determinant = gram_aa * gram_bb - gram_ab * gram_ab
    coef_a = (gram_bb * right_a - gram_ab * right_b) / determinant
    coef_b = (gram_aa * right_b - gram_ab * right_a) / determinant
    return spread(coef_a, first) + spread(coef_b, second)
```

```python
import math

import jax
import jax.numpy as jnp
from jax import lax
from jax.sharding import PartitionSpec as P


def extended_2(block, sides, width):
    for axis, dim in sides:
        count = lax.axis_size(axis)
        forward = [(i, i + 1) for i in range(count - 1)]
        backward = [(target, source) for source, target in forward]
        low = lax.ppermute(
            lax.slice_in_dim(block, block.shape[dim] - width, None, axis=dim), axis, forward
        )
        high = lax.ppermute(lax.slice_in_dim(block, 0, width, axis=dim), axis, backward)
        block = jnp.concatenate([low, block, high], axis=dim)
    return block


def slot_table(list_slot, list_class, classes):
    labels = jnp.arange(classes, dtype=jnp.int32)
    matches = list_class[:, :, None] == labels[None, None, :]
    return jnp.sum(jnp.where(matches, list_slot[:, :, None] + 1, 0), axis=1) - 1


def apply_classes(totals, operators, offset, table, received):
    count = operators.shape[0]
    picked = lax.dynamic_slice_in_dim(table, offset, count, 1)
    sources = jnp.where(
        (picked >= 0)[:, :, None, None],
        received[jnp.maximum(picked, 0)],
        jnp.zeros((), received.dtype),
    )
    return totals + jnp.einsum(
        "cqp,tcrp->trq", operators, sources, preferred_element_type=jnp.float32
    )


def fold_classes(totals, pieces, offset, table, received):
    count = pieces.shape[0]
    stride = math.gcd(count, 16)

    def step_once(number, current):
        operators = lax.dynamic_slice_in_dim(pieces, number * stride, stride, 0)
        return apply_classes(current, operators, offset + number * stride, table, received)

    return lax.fori_loop(0, count // stride, step_once, totals)


def inner(first, second):
    return jnp.sum(first * second, axis=(1, 2))


def spread(values, field):
    return values[:, None, None] * field


def per_device(
    rhs_field, self_coef, expand, near_ops, class_ops, near_src, send_rows, list_slot, list_class
):
    boxes = expand.shape[0]
    band = class_ops.shape[1]
    classes = class_ops.shape[0] * lax.axis_size("box")
    table = slot_table(list_slot, list_class, classes)
    level_index = lax.axis_index("level")
    cached = lax.all_gather(class_ops, "box", axis=0, tiled=True)

    def apply_matrix(field):
        field_half = field.astype(jnp.bfloat16)
        multipoles = jnp.einsum(
            "tpk,rtk->trp", expand, field_half, preferred_element_type=jnp.float32
        ).astype(jnp.bfloat16)
        outgoing = multipoles[send_rows[0]]
        received = lax.all_to_all(outgoing, "box", split_axis=0, concat_axis=0, tiled=True)
        received = received.reshape((-1,) + received.shape[2:])
        extended = extended_2(field_half, (("box", 1),), boxes)
        neighbours = extended[:, near_src]
        near_part = jnp.einsum(
            "kij,rtkj->rti", near_ops, neighbours, preferred_element_type=jnp.float32
        )
        empty = jnp.zeros((boxes, field.shape[0], band), jnp.float32)
        local_full = fold_classes(empty, cached, 0, table, received)
        local_half = local_full.astype(jnp.bfloat16)
        expand_rows = lax.dynamic_slice_in_dim(expand, level_index * band, band, 1)
        partial_field = jnp.einsum(
            "tqk,trq->rtk", expand_rows, local_half, preferred_element_type=jnp.float32
        )
        far_part = lax.psum(partial_field.astype(jnp.bfloat16), "level").astype(jnp.float32)
        return self_coef[None] * field + near_part + far_part

    def totals(*pairs):
        stacked = jnp.stack([inner(a, b) for a, b in pairs])
        return jnp.sum(lax.all_gather(stacked, "box"), axis=0)

    first_image = apply_matrix(rhs_field)
    rr, ra = totals((rhs_field, rhs_field), (rhs_field, first_image))
    h_one_one = ra / rr
    second = first_image - spread(h_one_one, rhs_field)
    second_image = apply_matrix(second)
    uu, rb, ub, bb = totals(
        (second, second),
        (rhs_field, second_image),
        (second, second_image),
        (second_image, second_image),
    )
    beta = jnp.sqrt(rr)
    length = jnp.sqrt(uu)
    h_two_one = length / beta
    h_one_two = rb / (beta * length)
    h_two_two = ub / uu
    gram_aa = h_one_one * h_one_one + h_two_one * h_two_one
    gram_ab = h_one_one * h_one_two + h_two_one * h_two_two
    gram_bb = bb / uu
    right_a = beta * h_one_one
    right_b = beta * h_one_two
    determinant = gram_aa * gram_bb - gram_ab * gram_ab
    coef_a = (gram_bb * right_a - gram_ab * right_b) / determinant
    coef_b = (gram_aa * right_b - gram_ab * right_a) / determinant
    return spread(coef_a / beta, rhs_field) + spread(coef_b / length, second)


def solution(mesh):
    return jax.shard_map(
        per_device,
        mesh=mesh,
        in_specs=(
            P(None, "box", None),
            P("box", None),
            P("box", None, None),
            P(),
            P("box", "level", None),
            P("box", None),
            P("box", None, None),
            P("box", None),
            P("box", None),
        ),
        out_specs=P(None, "box", None),
        check_vma=False,
    )
```

```python
import jax
import jax.numpy as jnp
from jax import lax
from jax.experimental import pallas as pl
from jax.experimental.pallas import tpu as pltpu
from jax.sharding import PartitionSpec as P

NZ, NY, NC, NX = 16, 4, 2, 4
NYC = NY * NC
SHIFT = 3.0
F32, BF16 = jnp.float32, jnp.bfloat16


def dot(a, b):
    return jnp.dot(a, b, preferred_element_type=F32)


def dot_nt(a, b):
    return lax.dot_general(a, b, (((1,), (1,)), ((), ())), preferred_element_type=F32)


def iota(shape, dim):
    return lax.broadcasted_iota(jnp.int32, shape, dim)


def body(
    rhs_ref, self_ref, expand_hbm, near_hbm, cls_ref, oh_ref, nearoh_ref, sendoh_ref,
    out_ref,
    efull, nops, tout, tin, wbuf, hbuf, obuf, zbuf, pbuf, rbuf, r2, g2, nbuf, xbuf,
    rz_out, rz, ry_out, ry,
    load_sem, t_send, t_recv, ring_send, ring_recv, y_send, y_recv, sib_send, sib_recv,
    h_send, h_recv, z_send, z_recv, p_send, p_recv, x_send, x_recv,
    rz_send, rz_recv, ry_send, ry_recv,
):
    me = lax.axis_index("box")
    x = lax.axis_index("level")
    z = me // NYC
    yc = me % NYC
    y = yc // NC
    core = yc % NC
    sends = []

    def start(src, dst, ssem, rsem, box, level):
        copy = pltpu.make_async_remote_copy(
            src_ref=src, dst_ref=dst, send_sem=ssem, recv_sem=rsem,
            device_id=(box, level), device_id_type=pl.DeviceIdType.MESH,
        )
        copy.start()
        sends.append(copy)

    def arrived(dst, rsem):
        pltpu.make_async_remote_copy(
            src_ref=dst, dst_ref=dst, send_sem=rsem, recv_sem=rsem,
            device_id=(me, x), device_id_type=pl.DeviceIdType.MESH,
        ).wait_recv()

    load_e = pltpu.make_async_copy(expand_hbm, efull, load_sem.at[0])
    load_n = pltpu.make_async_copy(near_hbm, nops, load_sem.at[1])
    load_e.start()
    load_n.start()

    def z_peer(d):
        return ((z + d) % NZ) * NYC + yc

    def p_peer(d):
        return z * NYC + (yc + d) % NYC

    def x_peer(d):
        return (x + d) % NX

    has_low = me > 0
    has_high = me < NZ * NYC - 1

    barrier = pltpu.get_barrier_semaphore()

    def greet(box, level):
        pl.semaphore_signal(
            barrier, inc=1, device_id=(box, level), device_id_type=pl.DeviceIdType.MESH
        )

    for d in range(1, NZ):
        greet(z_peer(d), x)
    for d in range(1, NYC):
        greet(p_peer(d), x)
    for d in range(1, NX):
        greet(me, x_peer(d))

    @pl.when(has_low)
    def _():
        greet(me - 1, x)

    @pl.when(has_high)
    def _():
        greet(me + 1, x)

    cls = cls_ref[...]
    eye2 = jnp.where(iota((64, 128), 0) == iota((64, 128), 1) % 64, 1.0, 0.0).astype(BF16)
    turned = lax.dot_general(
        cls, eye2, (((0,), (0,)), ((), ())), preferred_element_type=F32
    ).astype(BF16)
    tout[...] = turned.reshape(NX, 64, 128)

    pl.semaphore_wait(
        barrier,
        (NZ - 1) + (NYC - 1) + (NX - 1)
        + has_low.astype(jnp.int32) + has_high.astype(jnp.int32),
    )

    for d in range(1, NX):
        start(tout.at[x_peer(d)], tin.at[x], t_send.at[d], t_recv.at[x], me, x_peer(d))
    tin[x] = tout[x]

    lane128 = iota((16, 128), 1)
    low16 = lane128 < 64
    row_t = iota((16, 128), 0)
    rows64 = iota((64, 256), 0) % 16

    def halo_sends(it, v):
        half = v.astype(BF16)
        for r in range(4):
            hbuf[it, 1, :, r * 128:(r + 1) * 128] = half[r * 16:(r + 1) * 16]

        low = pltpu.make_async_remote_copy(
            src_ref=hbuf.at[it, 1], dst_ref=hbuf.at[it, 2],
            send_sem=h_send.at[it, 0], recv_sem=h_recv.at[it, 1],
            device_id=(me - 1, x), device_id_type=pl.DeviceIdType.MESH,
        )
        high = pltpu.make_async_remote_copy(
            src_ref=hbuf.at[it, 1], dst_ref=hbuf.at[it, 0],
            send_sem=h_send.at[it, 1], recv_sem=h_recv.at[it, 0],
            device_id=(me + 1, x), device_id_type=pl.DeviceIdType.MESH,
        )

        @pl.when(has_low)
        def _():
            low.start()

        @pl.when(has_high)
        def _():
            high.start()

        @pl.when(jnp.logical_not(has_low))
        def _():
            hbuf[it, 0] = jnp.zeros((16, 512), BF16)

        @pl.when(jnp.logical_not(has_high))
        def _():
            hbuf[it, 2] = jnp.zeros((16, 512), BF16)

        return half, low, high

    def multipole_sends(it, half):
        band = efull[:, pl.ds(pl.multiple_of(x * 64, 64), 64), :].reshape(1024, 128)
        full = dot_nt(half, band)
        doubled = []
        for r in range(4):
            total = jnp.zeros((16, 128), F32)
            for j in range(8):
                piece = full[r * 16:(r + 1) * 16, j * 128:(j + 1) * 128]
                total = total + jnp.where(
                    row_t == 2 * j + jnp.where(low16, 0, 1), piece, 0.0
                )
            doubled.append(total + pltpu.roll(total, 64, 1))
        rows = jnp.concatenate(
            [
                jnp.where(low16, doubled[0], doubled[1]),
                jnp.where(low16, doubled[2], doubled[3]),
            ],
            axis=1,
        ).astype(BF16)
        obuf[it] = dot(sendoh_ref[...], rows).astype(BF16).reshape(NZ, 16, 256)
        for d in (8, 7, 9, 6, 10, 5, 11, 4, 12, 3, 13, 2, 14, 1, 15):
            to = (z + d) % NZ
            start(obuf.at[it, to], zbuf.at[it, z], z_send.at[it, d], z_recv.at[it, z],
                  to * NYC + yc, x)
        zbuf[it, z] = obuf[it, z]

    def resort_sends(it):
        for d in range(1, NZ):
            src = (z + d) % NZ
            arrived(zbuf.at[it, src], z_recv.at[it, src])
        row = iota((256, 256), 0)
        want = ((row // 2) % 16) * 16 + (row // 32) * 2 + row % 2
        order = jnp.where(want == iota((256, 256), 1), 1.0, 0.0).astype(BF16)
        pbuf[it] = dot(order, zbuf[it].reshape(256, 256)).astype(BF16).reshape(8, 32, 256)
        for d in range(1, NYC):
            to = (yc + d) % NYC
            start(pbuf.at[it, to], rbuf.at[it, yc], p_send.at[it, d], p_recv.at[it, yc],
                  z * NYC + to, x)
        rbuf[it, yc] = pbuf[it, yc]

    def near_field(it, low, high):
        @pl.when(has_low)
        def _():
            high.wait_recv()

        @pl.when(has_high)
        def _():
            low.wait_recv()

        nbuf[...] = dot(nearoh_ref[...], hbuf[it].reshape(48, 512)).astype(BF16)

        def one(c, acc):
            rows = nbuf[pl.ds(pl.multiple_of(c * 16, 16), 16), :]
            lhs = jnp.concatenate([rows[:, r * 128:(r + 1) * 128] for r in range(4)], axis=0)
            return acc + dot_nt(lhs, nops[c])

        return lax.fori_loop(0, 26, one, jnp.zeros((64, 128), F32))

    def pick_sources(it):
        for d in range(1, NYC):
            src = (yc + d) % NYC
            arrived(rbuf.at[it, src], p_recv.at[it, src])
        low = iota((256, 128), 1) < 64
        received = rbuf[it].reshape(256, 256)
        for h in range(2):
            a = received[:, h * 128:(h + 1) * 128].astype(F32)
            b = pltpu.roll(a, 64, 1)
            for r, first, second in ((2 * h, a, b), (2 * h + 1, b, a)):
                lanes = slice(r * 128, (r + 1) * 128)
                r2[0:256, lanes] = jnp.where(low, first, 0.0).astype(BF16)
                r2[256:512, lanes] = jnp.where(low, 0.0, second).astype(BF16)

        def one(i, carry):
            at = pl.ds(pl.multiple_of(i * 128, 128), 128)
            g2[at, :] = dot(oh_ref[at, :], r2[...]).astype(BF16)
            return carry

        lax.fori_loop(0, 8, one, 0)

    def local_far_sends(it):
        def one(i, acc):
            rows = g2[pl.ds(pl.multiple_of(i * 32, 32), 32), :]
            lhs = jnp.concatenate(
                [
                    jnp.concatenate(
                        [rows[0:16, r * 128:(r + 1) * 128], rows[16:32, r * 128:(r + 1) * 128]],
                        axis=1,
                    )
                    for r in range(4)
                ],
                axis=0,
            )
            ops = wbuf[pl.ds(i * 4, 4)].reshape(256, 256)
            return acc + dot(lhs, ops)

        local = lax.fori_loop(0, 32, one, jnp.zeros((64, 256), F32))

        def far_one(t, acc):
            return acc + dot(jnp.where(rows64 == t, local, 0.0).astype(BF16), efull[t])

        far = lax.fori_loop(0, 16, far_one, jnp.zeros((64, 128), F32))
        xbuf[it, x] = far.astype(BF16)
        for d in range(1, NX):
            start(xbuf.at[it, x], xbuf.at[it, x], x_send.at[it, d], x_recv.at[it, x],
                  me, x_peer(d))

    def far_sum(it):
        for d in range(1, NX):
            arrived(xbuf.at[it, x_peer(d)], x_recv.at[it, x_peer(d)])
        total = xbuf[it, 0].astype(F32)
        for k in range(1, NX):
            total = total + xbuf[it, k].astype(F32)
        return total

    lane1 = iota((1, 128), 1)

    def packed(pairs):
        row = jnp.zeros((1, 128), F32)
        for q, (a, b) in enumerate(pairs):
            product = a * b
            for r in range(4):
                value = jnp.sum(
                    jnp.sum(product[r * 16:(r + 1) * 16], axis=0, keepdims=True),
                    axis=1, keepdims=True,
                )
                row = row + jnp.where(lane1 == q * 4 + r, value, 0.0)
        return row

    def reduce_z(it, row):
        rz_out[it] = row
        for d in range(1, NZ):
            start(rz_out.at[it], rz.at[it, z], rz_send.at[it, d], rz_recv.at[it, z],
                  z_peer(d), x)
        rz[it, z] = row

    def reduce_p(it):
        for d in range(1, NZ):
            src = (z + d) % NZ
            arrived(rz.at[it, src], rz_recv.at[it, src])
        row = jnp.sum(rz[it], axis=0)
        ry_out[it] = row
        for d in range(1, NYC):
            start(ry_out.at[it], ry.at[it, yc], ry_send.at[it, d], ry_recv.at[it, yc],
                  p_peer(d), x)
        ry[it, yc] = row

    def reduced(it):
        for d in range(1, NYC):
            src = (yc + d) % NYC
            arrived(ry.at[it, src], ry_recv.at[it, src])
        return jnp.sum(ry[it], axis=0)

    def spread(row):
        return jnp.concatenate(
            [
                jnp.broadcast_to(
                    jnp.sum(jnp.where(lane1 == r, row, 0.0), axis=1, keepdims=True), (16, 128)
                )
                for r in range(4)
            ],
            axis=0,
        )

    v = rhs_ref[...].reshape(64, 128)
    diag = jnp.concatenate([self_ref[...]] * 4, axis=0)
    half, low_copy, high_copy = halo_sends(0, v)
    load_e.wait()
    multipole_sends(0, half)

    for d in range(1, NX):
        arrived(tin.at[x_peer(d)], t_recv.at[x_peer(d)])
    low_t = iota((64, 128), 1) < 64
    pairs = [
        jnp.where(low_t, tin[2 * h].astype(F32), tin[2 * h + 1].astype(F32)) for h in range(2)
    ]
    wbuf[me] = jnp.concatenate(pairs, axis=1).astype(BF16)

    def cls_at(m, y_rel):
        return wbuf.at[((z - m + NZ) % NZ) * NYC + ((y + y_rel) % NY) * NC + core]

    def ring(m_at, step, right):
        ref = cls_at(m_at, 0)
        way = 0 if right else 1
        start(ref, ref, ring_send.at[way, step], ring_recv.at[way, step],
              z_peer(1 if right else NZ - 1), x)

    def y_out(m):
        ref = cls_at(m, 0)
        up = z * NYC + ((y + 1) % NY) * NC + core
        down = z * NYC + ((y + 3) % NY) * NC + core
        start(ref, ref, y_send.at[0, m], y_recv.at[0, m], up, x)
        start(ref, ref, y_send.at[1, m], y_recv.at[1, m], down, x)

    def sibling(m, y_rel):
        ref = cls_at(m, y_rel)
        start(ref, ref, sib_send.at[y_rel, m], sib_recv, z * NYC + y * NC + 1 - core, x)

    def y_in(m):
        arrived(cls_at(m, 3), y_recv.at[0, m])
        arrived(cls_at(m, 1), y_recv.at[1, m])
        if m % 2 == 0:
            ref = cls_at(m, 3)
            to = z * NYC + ((y + 1) % NY) * NC + core
        else:
            ref = cls_at(m, 1)
            to = z * NYC + ((y + 3) % NY) * NC + core
        start(ref, ref, y_send.at[2, m], y_recv.at[2, m], to, x)
        sibling(m, 3)
        sibling(m, 1)

    def y_far_in(m):
        arrived(cls_at(m, 2), y_recv.at[2, m])
        sibling(m, 2)

    def step_set(k):
        if k == 0:
            return [0]
        if k == 8:
            return [8]
        return [k, NZ - k]

    ring(0, 1, True)
    ring(0, 1, False)
    y_out(0)
    sibling(0, 0)

    load_n.wait()
    near_one = near_field(0, low_copy, high_copy)

    for k in range(1, 9):
        arrived(cls_at(k, 0), ring_recv.at[0, k])
        if k < 8:
            ring(k, k + 1, True)
            arrived(cls_at(NZ - k, 0), ring_recv.at[1, k])
            if k < 7:
                ring(NZ - k, k + 1, False)
        for m in step_set(k):
            y_out(m)
            sibling(m, 0)
        for m in step_set(k - 1):
            y_in(m)
        if k >= 2:
            for m in step_set(k - 2):
                y_far_in(m)
        if k == 3:
            resort_sends(0)
        if k == 6:
            pick_sources(0)
    for m in step_set(8):
        y_in(m)
    for k in (7, 8):
        for m in step_set(k):
            y_far_in(m)
    other = wbuf.at[pl.ds(0, 64)]
    arrived(other, sib_recv)

    local_far_sends(0)
    base = diag * v + near_one
    image = base + far_sum(0)

    shifted = image - SHIFT * v
    half, low_two, high_two = halo_sends(1, shifted)
    multipole_sends(1, half)
    reduce_z(0, packed([(v, v), (v, image)]))
    near_two = near_field(1, low_two, high_two)
    resort_sends(1)
    reduce_p(0)
    pick_sources(1)
    local_far_sends(1)

    first_sums = reduced(0)
    rr = first_sums
    ra = pltpu.roll(first_sums, 124, 1)
    h11 = ra / rr
    slope = spread(h11)
    u = image - slope * v
    base = diag * shifted + near_two - (slope - SHIFT) * image
    b = base + far_sum(1)
    reduce_z(1, packed([(u, u), (v, b), (u, b), (b, b)]))
    reduce_p(1)
    second_sums = reduced(1)
    uu = second_sums
    rb = pltpu.roll(second_sums, 124, 1)
    ub = pltpu.roll(second_sums, 120, 1)
    bb = pltpu.roll(second_sums, 116, 1)
    beta = jnp.sqrt(rr)
    length = jnp.sqrt(uu)
    h21 = length / beta
    h12 = rb / (beta * length)
    h22 = ub / uu
    gram_aa = h11 * h11 + h21 * h21
    gram_ab = h11 * h12 + h21 * h22
    gram_bb = bb / uu
    right_a = beta * h11
    right_b = beta * h12
    det = gram_aa * gram_bb - gram_ab * gram_ab
    coef_a = (gram_bb * right_a - gram_ab * right_b) / det / beta
    coef_b = (gram_aa * right_b - gram_ab * right_a) / det / length
    out_ref[...] = (spread(coef_a) * v + spread(coef_b) * u).reshape(4, 16, 128)

    for copy in sends:
        copy.wait_send()
    for low, high in ((low_copy, high_copy), (low_two, high_two)):
        @pl.when(has_low)
        def _():
            low.wait_send()

        @pl.when(has_high)
        def _():
            high.wait_send()


def per_device(
    rhs_field, self_coef, expand, near_ops, class_ops, near_src, send_rows, list_slot, list_class
):
    slot = ((list_slot // 2) % 8) * 32 + (list_slot // 16) * 2 + list_slot % 2
    labels = jnp.arange(128, dtype=jnp.int32)
    matches = list_class[:, None, :] == labels[None, :, None]
    table = jnp.sum(jnp.where(matches, slot[:, None, :] + 1, 0), axis=2) - 1
    table = table.T.reshape(64, 2, 16).transpose(0, 2, 1).reshape(1024, 2, 1)
    hot = (table == jnp.arange(256, dtype=jnp.int32)).astype(BF16).reshape(1024, 512)
    near_hot = (
        near_src.T.reshape(416, 1) == jnp.arange(48, dtype=jnp.int32)
    ).astype(BF16)
    send_hot = (
        send_rows[0].reshape(256, 1) == jnp.arange(16, dtype=jnp.int32)
    ).astype(BF16)

    vmem = pl.BlockSpec(memory_space=pltpu.VMEM)
    hbm = pl.BlockSpec(memory_space=pl.ANY)
    dma = pltpu.SemaphoreType.DMA
    return pl.pallas_call(
        body,
        out_shape=jax.ShapeDtypeStruct((4, 16, 128), F32),
        in_specs=[vmem, vmem, hbm, hbm, vmem, vmem, vmem, vmem],
        out_specs=vmem,
        scratch_shapes=[
            pltpu.VMEM((16, 256, 128), BF16),
            pltpu.VMEM((26, 128, 128), BF16),
            pltpu.VMEM((NX, 64, 128), BF16),
            pltpu.VMEM((NX, 64, 128), BF16),
            pltpu.VMEM((128, 64, 256), BF16),
            pltpu.VMEM((2, 3, 16, 512), BF16),
            pltpu.VMEM((2, NZ, 16, 256), BF16),
            pltpu.VMEM((2, NZ, 16, 256), BF16),
            pltpu.VMEM((2, NYC, 32, 256), BF16),
            pltpu.VMEM((2, NYC, 32, 256), BF16),
            pltpu.VMEM((512, 512), BF16),
            pltpu.VMEM((1024, 512), BF16),
            pltpu.VMEM((416, 512), BF16),
            pltpu.VMEM((2, NX, 64, 128), BF16),
            pltpu.VMEM((2, 1, 128), F32),
            pltpu.VMEM((2, NZ, 1, 128), F32),
            pltpu.VMEM((2, 1, 128), F32),
            pltpu.VMEM((2, NYC, 1, 128), F32),
            dma((2,)),
            dma((NX,)), dma((NX,)),
            dma((2, 9)), dma((2, 9)),
            dma((3, NZ)), dma((3, NZ)),
            dma((NY, NZ)), dma,
            dma((2, 2)), dma((2, 2)),
            dma((2, NZ)), dma((2, NZ)),
            dma((2, NYC)), dma((2, NYC)),
            dma((2, NX)), dma((2, NX)),
            dma((2, NZ)), dma((2, NZ)),
            dma((2, NYC)), dma((2, NYC)),
        ],
        compiler_params=pltpu.CompilerParams(
            collective_id=0, has_side_effects=True, vmem_limit_bytes=40 * 1024 * 1024
        ),
        cost_estimate=pl.CostEstimate(
            flops=4_000_000_000, bytes_accessed=4_000_000, transcendentals=0
        ),
    )(
        rhs_field, self_coef, expand, near_ops, class_ops[0], hot, near_hot, send_hot
    )


def solution(mesh):
    return jax.shard_map(
        per_device,
        mesh=mesh,
        in_specs=(
            P(None, "box", None),
            P("box", None),
            P("box", None, None),
            P(),
            P("box", "level", None),
            P("box", None),
            P("box", None, None),
            P("box", None),
            P("box", None),
        ),
        out_specs=P(None, "box", None),
        check_vma=False,
    )
```

```python
import jax
import jax.numpy as jnp
from jax import lax
from jax.experimental import pallas as pl
from jax.experimental.pallas import tpu as pltpu
from jax.sharding import PartitionSpec as P

NZ, NY, NC, NX = 16, 4, 2, 4
NYC = NY * NC
SHIFT = 3.0
RADIUS = 3
NBOX_DEV = NZ * NYC
F32, BF16 = jnp.float32, jnp.bfloat16


def dot(a, b):
    return jnp.dot(a, b, preferred_element_type=F32)


def dot_nt(a, b):
    return lax.dot_general(a, b, (((1,), (1,)), ((), ())), preferred_element_type=F32)


def iota(shape, dim):
    return lax.broadcasted_iota(jnp.int32, shape, dim)


def peer_offsets():
    offsets = [
        (dz, dy, dc) for dz in range(NZ) for dy in range(NY) for dc in range(NC)
        if (dz, dy, dc) != (0, 0, 0)
    ]
    return sorted(offsets, key=lambda o: -(2 * min(o[0], NZ - o[0]) + 2 * min(o[1], NY - o[1]) + o[2]))


def body(
    rhs_hbm, self_hbm, expand_hbm, near_hbm, cls_hbm, near_src_hbm, rows_hbm, slot_hbm, class_hbm,
    out_ref,
    rhs_ref, self_ref, cls_ref, near_src_ref, rows_ref, slot_ref, class_ref,
    efull, nops, tout, tin, wbuf, hbuf, obuf, rbuf, r2, g2, nbuf, xbuf, tab, oh, nearoh, sendoh,
    rz_out, rz, ry_out, ry, ra_out, rall,
    load_sem, t_send, t_recv, ring_send, ring_recv, y_send, y_recv, sib_send, sib_recv,
    h_send, h_recv, a_send, a_recv, x_send, x_recv,
    rz_send, rz_recv, ry_send, ry_recv, ra_send, ra_recv,
):
    me = lax.axis_index("box")
    x = lax.axis_index("level")
    z = me // NYC
    yc = me % NYC
    y = yc // NC
    core = yc % NC
    sends = []
    mesh_ids = pl.DeviceIdType.MESH

    def remote(src, dst, ssem, rsem, box, level):
        return pltpu.make_async_remote_copy(
            src_ref=src, dst_ref=dst, send_sem=ssem, recv_sem=rsem,
            device_id=(box, level), device_id_type=mesh_ids,
        )

    def start(src, dst, ssem, rsem, box, level):
        copy = remote(src, dst, ssem, rsem, box, level)
        copy.start()
        sends.append(copy)

    def arrived(dst, rsem):
        remote(dst, dst, rsem, rsem, me, x).wait_recv()

    def sent(ref, ssem):
        remote(ref, ref, ssem, ssem, me, x).wait_send()

    def settle():
        for copy in sends:
            copy.wait_send()
        sends.clear()

    def box_at(offset):
        dz, dy, dc = offset
        return ((z + dz) % NZ) * NYC + ((y + dy) % NY) * NC + (core + dc) % NC

    def z_peer(d):
        return ((z + d) % NZ) * NYC + yc

    def p_peer(d):
        return z * NYC + (yc + d) % NYC

    def x_peer(d):
        return (x + d) % NX

    has_low = me > 0
    has_high = me < NBOX_DEV - 1

    barrier = pltpu.get_barrier_semaphore()
    offsets = peer_offsets()
    for offset in offsets:
        pl.semaphore_signal(barrier, inc=1, device_id=(box_at(offset), x), device_id_type=mesh_ids)
    for d in range(1, NX):
        pl.semaphore_signal(barrier, inc=1, device_id=(me, x_peer(d)), device_id_type=mesh_ids)

    loads = [
        pltpu.make_async_copy(src, dst, load_sem.at[i])
        for i, (src, dst) in enumerate((
            (cls_hbm, cls_ref), (rows_hbm, rows_ref), (rhs_hbm, rhs_ref), (expand_hbm, efull),
            (self_hbm, self_ref), (slot_hbm, slot_ref), (class_hbm, class_ref),
            (near_src_hbm, near_src_ref), (near_hbm, nops),
        ))
    ]
    for load in loads:
        load.start()
    loads[0].wait()

    eye2 = jnp.where(iota((64, 128), 0) == iota((64, 128), 1) % 64, 1.0, 0.0).astype(BF16)
    turned = lax.dot_general(
        cls_ref[...], eye2, (((0,), (0,)), ((), ())), preferred_element_type=F32
    ).astype(BF16)
    tout[...] = turned.reshape(NX, 64, 128)
    tin[x] = tout[x]

    loads[1].wait()
    for j in range(2):
        hot = jnp.where(iota((128, 128), 0) == rows_ref[j:j + 1, :], 1.0, 0.0)
        tab[pl.ds(j, 128, stride=2), :] = hot.T
    sendoh[...] = tab[0:256, :].astype(BF16)

    lane128 = iota((16, 128), 1)
    low16 = lane128 < 64
    row_t = iota((16, 128), 0)
    rows64 = iota((64, 256), 0) % 16

    def halo_fill(it, v):
        half = v.astype(BF16)
        for r in range(4):
            hbuf[it, 1, :, r * 128:(r + 1) * 128] = half[r * 16:(r + 1) * 16]
        return half

    def halo_sends(it):
        low = remote(hbuf.at[it, 1], hbuf.at[it, 2], h_send.at[it, 0], h_recv.at[it, 1], me - 1, x)
        high = remote(hbuf.at[it, 1], hbuf.at[it, 0], h_send.at[it, 1], h_recv.at[it, 0], me + 1, x)

        @pl.when(has_low)
        def _():
            low.start()

        @pl.when(has_high)
        def _():
            high.start()

        @pl.when(jnp.logical_not(has_low))
        def _():
            hbuf[it, 0] = jnp.zeros((16, 512), BF16)

        @pl.when(jnp.logical_not(has_high))
        def _():
            hbuf[it, 2] = jnp.zeros((16, 512), BF16)

        return low, high

    def halo_settle(low, high):
        @pl.when(has_low)
        def _():
            low.wait_send()

        @pl.when(has_high)
        def _():
            high.wait_send()

    def multipoles(it, half):
        band = efull[:, pl.ds(pl.multiple_of(x * 64, 64), 64), :].reshape(1024, 128)
        full = dot_nt(half, band)
        doubled = []
        for r in range(4):
            total = jnp.zeros((16, 128), F32)
            for j in range(8):
                piece = full[r * 16:(r + 1) * 16, j * 128:(j + 1) * 128]
                total = total + jnp.where(
                    row_t == 2 * j + jnp.where(low16, 0, 1), piece, 0.0
                )
            doubled.append(total + pltpu.roll(total, 64, 1))
        for h in range(2):
            rows = jnp.where(low16, doubled[2 * h], doubled[2 * h + 1]).astype(BF16)
            picked = dot(sendoh[:, 0:16], rows)
            obuf[it, h] = picked.astype(BF16).reshape(NBOX_DEV, 2, 128)

    def multipole_sends(it):
        for offset in offsets:
            to = box_at(offset)
            remote(obuf.at[it, :, to], rbuf.at[it, :, me], a_send.at[it], a_recv.at[it],
                   to, x).start()
        rbuf[it, :, me] = obuf[it, :, me]

    def many(it):
        return rbuf.at[it, :, pl.ds(0, NBOX_DEV - 1)]

    def near_field(it, low, high):
        @pl.when(has_low)
        def _():
            high.wait_recv()

        @pl.when(has_high)
        def _():
            low.wait_recv()

        nbuf[...] = dot(nearoh[...], hbuf[it].reshape(48, 512)).astype(BF16)

        def one(c, acc):
            rows = nbuf[pl.ds(pl.multiple_of(c * 16, 16), 16), :]
            lhs = jnp.concatenate([rows[:, r * 128:(r + 1) * 128] for r in range(4)], axis=0)
            return acc + dot_nt(lhs, nops[c])

        return lax.fori_loop(0, 26, one, jnp.zeros((64, 128), F32), unroll=2)

    def pick_sources(it):
        arrived(many(it), a_recv.at[it])
        low = iota((256, 128), 1) < 64
        for h in range(2):
            a = rbuf[it, h].reshape(256, 128).astype(F32)
            b = pltpu.roll(a, 64, 1)
            for r, first, second in ((2 * h, a, b), (2 * h + 1, b, a)):
                lanes = slice(r * 128, (r + 1) * 128)
                r2[0:256, lanes] = jnp.where(low, first, 0.0).astype(BF16)
                r2[256:512, lanes] = jnp.where(low, 0.0, second).astype(BF16)

        for i in range(4):
            picked = dot(oh[i * 256:(i + 1) * 256, :], r2[...]).astype(BF16)
            for k in range(16):
                for r in range(4):
                    g2[r * 16:(r + 1) * 16, (i * 16 + k) * 128:(i * 16 + k + 1) * 128] = (
                        picked[k * 16:(k + 1) * 16, r * 128:(r + 1) * 128]
                    )

    def local_far_sends(it):
        local = dot(g2[...], wbuf[...].reshape(8192, 256))
        far = jnp.zeros((64, 128), F32)
        for t in range(16):
            far = far + dot(jnp.where(rows64 == t, local, 0.0).astype(BF16), efull[t])
        xbuf[it, x] = far.astype(BF16)
        for d in (2, 1, 3):
            start(xbuf.at[it, x], xbuf.at[it, x], x_send.at[it, d], x_recv.at[it, x],
                  me, x_peer(d))

    def far_sum(it):
        for d in range(1, NX):
            arrived(xbuf.at[it, x_peer(d)], x_recv.at[it, x_peer(d)])
        total = xbuf[it, 0].astype(F32)
        for k in range(1, NX):
            total = total + xbuf[it, k].astype(F32)
        return total

    lane1 = iota((1, 128), 1)

    def packed(pairs):
        rows = []
        for a, b in pairs:
            product = a * b
            for r in range(4):
                rows.append(jnp.sum(product[r * 16:(r + 1) * 16], axis=0, keepdims=True))
        stacked = jnp.concatenate(rows, axis=0)
        sums = jnp.sum(stacked, axis=1, keepdims=True)
        shape = (len(rows), 128)
        return jnp.sum(
            jnp.where(iota(shape, 0) == iota(shape, 1), sums, 0.0), axis=0, keepdims=True
        )

    def reduce_z(row):
        rz_out[...] = row
        for d in range(1, NZ):
            start(rz_out, rz.at[z], rz_send.at[d], rz_recv.at[z], z_peer(d), x)
        rz[z] = row

    def reduce_p():
        for d in range(1, NZ):
            src = (z + d) % NZ
            arrived(rz.at[src], rz_recv.at[src])
        row = jnp.sum(rz[...], axis=0)
        ry_out[...] = row
        for d in range(1, NYC):
            start(ry_out, ry.at[yc], ry_send.at[d], ry_recv.at[yc], p_peer(d), x)
        ry[yc] = row

    def reduced():
        for d in range(1, NYC):
            src = (yc + d) % NYC
            arrived(ry.at[src], ry_recv.at[src])
        return jnp.sum(ry[...], axis=0)

    def reduce_all(row):
        ra_out[...] = row
        for offset in offsets:
            remote(ra_out, rall.at[me], ra_send, ra_recv, box_at(offset), x).start()
        rall[me] = row
        arrived(rall.at[pl.ds(0, NBOX_DEV - 1)], ra_recv)
        return jnp.sum(rall[...], axis=0)

    def spread(row):
        return jnp.concatenate(
            [
                jnp.broadcast_to(
                    jnp.sum(jnp.where(lane1 == r, row, 0.0), axis=1, keepdims=True), (16, 128)
                )
                for r in range(4)
            ],
            axis=0,
        )

    loads[2].wait()
    loads[4].wait()
    v = rhs_ref[...].reshape(64, 128)
    diag = jnp.concatenate([self_ref[...]] * 4, axis=0)
    half = halo_fill(0, v)
    loads[3].wait()
    multipoles(0, half)

    pl.semaphore_wait(barrier, NBOX_DEV - 1 + NX - 1)

    for d in (2, 1, 3):
        start(tout.at[x_peer(d)], tin.at[x], t_send.at[d], t_recv.at[x], me, x_peer(d))
    low_copy, high_copy = halo_sends(0)
    multipole_sends(0)

    iota_c = iota((128, 64), 0)
    for load in loads[5:8]:
        load.wait()
    for t in range(16):
        match = iota_c == class_ref[t:t + 1, :]
        value = jnp.where(match, (slot_ref[t:t + 1, :] + 1).astype(F32), 0.0)
        tab[pl.ds(t, 128, stride=16), :] = jnp.broadcast_to(
            jnp.sum(value, axis=1, keepdims=True), (128, 128)
        )

    for d in range(1, NX):
        arrived(tin.at[x_peer(d)], t_recv.at[x_peer(d)])
    low_t = iota((64, 128), 1) < 64
    merged = [
        jnp.where(low_t, tin[2 * h].astype(F32), tin[2 * h + 1].astype(F32)) for h in range(2)
    ]
    wbuf[me] = jnp.concatenate(merged, axis=1).astype(BF16)

    def cls_at(m, y_rel):
        return wbuf.at[((z - m + NZ) % NZ) * NYC + ((y + y_rel) % NY) * NC + core]

    def relay(m, reach):
        ref = cls_at(m, 0)
        ways = ((0, 1), (1, -1)) if m == 0 else (((0, 1),) if m <= NZ // 2 else ((1, -1),))
        gone = m if m <= NZ // 2 else NZ - m
        for d in range(RADIUS, 0, -1):
            for way, sign in ways:
                at = gone + d
                if at <= reach[way]:
                    start(ref, ref, ring_send.at[way, at], ring_recv.at[way, at],
                          z_peer(sign * d % NZ), x)

    reach = (NZ // 2, NZ // 2 - 1)

    def y_out(m):
        ref = cls_at(m, 0)
        up = z * NYC + ((y + 1) % NY) * NC + core
        down = z * NYC + ((y + 3) % NY) * NC + core
        start(ref, ref, y_send.at[0, m], y_recv.at[0, m], up, x)
        start(ref, ref, y_send.at[1, m], y_recv.at[1, m], down, x)

    def sibling(m, y_rel):
        ref = cls_at(m, y_rel)
        start(ref, ref, sib_send.at[y_rel, m], sib_recv, z * NYC + y * NC + 1 - core, x)

    def z_in(m):
        gone = m if m <= NZ // 2 else NZ - m
        way = 0 if m <= NZ // 2 else 1
        arrived(cls_at(m, 0), ring_recv.at[way, gone])
        if gone % RADIUS == 0:
            relay(m, reach)
        y_out(m)
        sibling(m, 0)

    def y_in(m):
        arrived(cls_at(m, 3), y_recv.at[0, m])
        arrived(cls_at(m, 1), y_recv.at[1, m])
        if m % 2 == 0:
            ref = cls_at(m, 3)
            to = z * NYC + ((y + 1) % NY) * NC + core
        else:
            ref = cls_at(m, 1)
            to = z * NYC + ((y + 3) % NY) * NC + core
        start(ref, ref, y_send.at[2, m], y_recv.at[2, m], to, x)
        sibling(m, 3)
        sibling(m, 1)

    def y_far_in(m):
        arrived(cls_at(m, 2), y_recv.at[2, m])
        sibling(m, 2)

    relay(0, reach)
    y_out(0)
    sibling(0, 0)

    def hot_rows(i, carry):
        at = pl.multiple_of(i * 32, 32)
        for k in range(2):
            want = tab[pl.ds(at + k * 16, 16), :]
            for part in range(2):
                slots = (lane128 + (part * 128 + 1)).astype(F32)
                oh[pl.ds(pl.multiple_of(i * 16, 16), 16),
                   k * 256 + part * 128:k * 256 + (part + 1) * 128] = jnp.where(
                       want == slots, 1.0, 0.0).astype(BF16)
        return carry

    lax.fori_loop(0, 64, hot_rows, 0, unroll=4)
    for c in range(26):
        nearoh[c * 16:(c + 1) * 16, :] = jnp.where(
            near_src_ref[:, c:c + 1] == iota((16, 48), 1), 1.0, 0.0
        ).astype(BF16)

    loads[8].wait()
    near_one = near_field(0, low_copy, high_copy)

    for m in (3, 13, 1, 15, 2, 14):
        z_in(m)
    y_in(0)
    for m in (6, 10):
        z_in(m)
    for m in (3, 13):
        y_in(m)
    for m in (4, 12, 5, 11):
        z_in(m)
    for m in (1, 15, 2, 14):
        y_in(m)
    y_far_in(0)
    for m in (8, 7, 9):
        z_in(m)
    pick_sources(0)
    for m in (6, 10, 4, 12, 5, 11):
        y_in(m)
    for m in (3, 13, 1, 15, 2, 14):
        y_far_in(m)
    for m in (8, 7, 9):
        y_in(m)
    for m in (6, 10, 4, 12, 5, 11, 8, 7, 9):
        y_far_in(m)
    arrived(wbuf.at[pl.ds(0, NBOX_DEV // 2)], sib_recv)

    local_far_sends(0)
    base = diag * v + near_one
    image = base + far_sum(0)

    shifted = image - SHIFT * v
    half = halo_fill(1, shifted)
    multipoles(1, half)
    multipole_sends(1)
    low_two, high_two = halo_sends(1)
    reduce_z(packed([(v, v), (v, image)]))
    near_two = near_field(1, low_two, high_two)
    sent(many(0), a_send.at[0])
    halo_settle(low_copy, high_copy)
    reduce_p()
    pick_sources(1)
    local_far_sends(1)

    rr = reduced()
    ra = pltpu.roll(rr, 124, 1)
    h11 = ra / rr
    slope = spread(h11)
    u = image - slope * v
    base = diag * shifted + near_two - (slope - SHIFT) * image
    settle()
    halo_settle(low_two, high_two)
    sent(many(1), a_send.at[1])
    b = base + far_sum(1)
    uu = reduce_all(packed([(u, u), (v, b), (u, b), (b, b)]))
    rb = pltpu.roll(uu, 124, 1)
    ub = pltpu.roll(uu, 120, 1)
    bb = pltpu.roll(uu, 116, 1)
    beta = jnp.sqrt(rr)
    length = jnp.sqrt(uu)
    h21 = length / beta
    h12 = rb / (beta * length)
    h22 = ub / uu
    gram_aa = h11 * h11 + h21 * h21
    gram_ab = h11 * h12 + h21 * h22
    gram_bb = bb / uu
    right_a = beta * h11
    right_b = beta * h12
    det = gram_aa * gram_bb - gram_ab * gram_ab
    coef_a = (gram_bb * right_a - gram_ab * right_b) / det / beta
    coef_b = (gram_aa * right_b - gram_ab * right_a) / det / length
    out_ref[...] = (spread(coef_a) * v + spread(coef_b) * u).reshape(4, 16, 128)
    sent(rall.at[pl.ds(0, NBOX_DEV - 1)], ra_send)


def per_device(
    rhs_field, self_coef, expand, near_ops, class_ops, near_src, send_rows, list_slot, list_class
):
    vmem = pl.BlockSpec(memory_space=pltpu.VMEM)
    hbm = pl.BlockSpec(memory_space=pltpu.HBM)
    dma = pltpu.SemaphoreType.DMA
    return pl.pallas_call(
        body,
        out_shape=jax.ShapeDtypeStruct((4, 16, 128), F32),
        in_specs=[hbm] * 9,
        out_specs=vmem,
        scratch_shapes=[
            pltpu.VMEM((4, 16, 128), F32),
            pltpu.VMEM((16, 128), F32),
            pltpu.VMEM((64, 256), BF16),
            pltpu.VMEM((16, 26), jnp.int32),
            pltpu.VMEM((2, 128), jnp.int32),
            pltpu.VMEM((16, 64), jnp.int32),
            pltpu.VMEM((16, 64), jnp.int32),
            pltpu.VMEM((16, 256, 128), BF16),
            pltpu.VMEM((26, 128, 128), BF16),
            pltpu.VMEM((NX, 64, 128), BF16),
            pltpu.VMEM((NX, 64, 128), BF16),
            pltpu.VMEM((NBOX_DEV, 64, 256), BF16),
            pltpu.VMEM((2, 3, 16, 512), BF16),
            pltpu.VMEM((2, 2, NBOX_DEV, 2, 128), BF16),
            pltpu.VMEM((2, 2, NBOX_DEV, 2, 128), BF16),
            pltpu.VMEM((512, 512), BF16),
            pltpu.VMEM((64, 8192), BF16),
            pltpu.VMEM((416, 512), BF16),
            pltpu.VMEM((2, NX, 64, 128), BF16),
            pltpu.VMEM((2048, 128), F32),
            pltpu.VMEM((1024, 512), BF16),
            pltpu.VMEM((416, 48), BF16),
            pltpu.VMEM((256, 128), BF16),
            pltpu.VMEM((1, 128), F32),
            pltpu.VMEM((NZ, 1, 128), F32),
            pltpu.VMEM((1, 128), F32),
            pltpu.VMEM((NYC, 1, 128), F32),
            pltpu.VMEM((1, 128), F32),
            pltpu.VMEM((NBOX_DEV, 1, 128), F32),
            dma((9,)),
            dma((NX,)), dma((NX,)),
            dma((2, 9)), dma((2, 9)),
            dma((3, NZ)), dma((3, NZ)),
            dma((NY, NZ)), dma,
            dma((2, 2)), dma((2, 2)),
            dma((2,)), dma((2,)),
            dma((2, NX)), dma((2, NX)),
            dma((NZ,)), dma((NZ,)),
            dma((NYC,)), dma((NYC,)),
            dma, dma,
        ],
        compiler_params=pltpu.CompilerParams(
            collective_id=0, has_side_effects=True, vmem_limit_bytes=62 * 1024 * 1024
        ),
        cost_estimate=pl.CostEstimate(
            flops=4_000_000_000, bytes_accessed=4_000_000, transcendentals=0
        ),
    )(
        rhs_field, self_coef, expand, near_ops, class_ops[0], near_src, send_rows[0].T,
        list_slot, list_class,
    )


def solution(mesh):
    return jax.shard_map(
        per_device,
        mesh=mesh,
        in_specs=(
            P(None, "box", None),
            P("box", None),
            P("box", None, None),
            P(),
            P("box", "level", None),
            P("box", None),
            P("box", None, None),
            P("box", None),
            P("box", None),
        ),
        out_specs=P(None, "box", None),
        check_vma=False,
    )
```

```python
import jax
import jax.numpy as jnp
from jax import lax
from jax.experimental import pallas as pl
from jax.experimental.pallas import tpu as pltpu
from jax.sharding import PartitionSpec as P

NZ, NY, NC, NX = 16, 4, 2, 4
NYC = NY * NC
SHIFT = 3.0
RADIUS = 3
HOP = 2
FAR_DIRECT = (7, 8, 9)
EARLY = (0, 1, 15, 2, 14, 3, 13, 4, 12)
LATE = (5, 11, 6, 10, 7, 9, 8)
NBOX_DEV = NZ * NYC
F32, BF16 = jnp.float32, jnp.bfloat16


def dot(a, b):
    return jnp.dot(a, b, preferred_element_type=F32)


def dot_nt(a, b):
    return lax.dot_general(a, b, (((1,), (1,)), ((), ())), preferred_element_type=F32)


def iota(shape, dim):
    return lax.broadcasted_iota(jnp.int32, shape, dim)


def peer_offsets():
    offsets = [
        (dz, dy, dc) for dz in range(NZ) for dy in range(NY) for dc in range(NC)
        if (dz, dy, dc) != (0, 0, 0)
    ]
    return sorted(offsets, key=lambda o: -(2 * min(o[0], NZ - o[0]) + 2 * min(o[1], NY - o[1]) + o[2]))


def body(
    rhs_hbm, self_hbm, expand_hbm, near_hbm, cls_hbm, near_src_hbm, rows_hbm, slot_hbm, class_hbm,
    out_ref,
    rhs_ref, self_ref, cls_ref, near_src_ref, rows_ref, slot_ref, class_ref,
    efull, nops, tout, tin, wbuf, hbuf, obuf, rbuf, r2, g2, nbuf, xbuf, tab, oh, nearoh, sendoh,
    rz_out, rz, ry_out, ry, ra_out, rall,
    load_sem, t_send, t_recv, ring_send, ring_recv, y_send, y_recv, sib_send, sib_recv,
    h_send, h_recv, a_send, a_recv, x_send, x_recv,
    rz_send, rz_recv, ry_send, ry_recv, ra_send, ra_recv, known,
):
    me = lax.axis_index("box")
    x = lax.axis_index("level")
    z = me // NYC
    yc = me % NYC
    y = yc // NC
    core = yc % NC
    sends = []
    mesh_ids = pl.DeviceIdType.MESH

    def remote(src, dst, ssem, rsem, box, level):
        return pltpu.make_async_remote_copy(
            src_ref=src, dst_ref=dst, send_sem=ssem, recv_sem=rsem,
            device_id=(box, level), device_id_type=mesh_ids,
        )

    def start(src, dst, ssem, rsem, box, level):
        copy = remote(src, dst, ssem, rsem, box, level)
        copy.start()
        sends.append(copy)

    def arrived(dst, rsem):
        remote(dst, dst, rsem, rsem, me, x).wait_recv()

    def sent(ref, ssem):
        remote(ref, ref, ssem, ssem, me, x).wait_send()

    def settle():
        for copy in sends:
            copy.wait_send()
        sends.clear()

    def box_at(offset):
        dz, dy, dc = offset
        return ((z + dz) % NZ) * NYC + ((y + dy) % NY) * NC + (core + dc) % NC

    def z_peer(d):
        return ((z + d) % NZ) * NYC + yc

    def p_peer(d):
        return z * NYC + (yc + d) % NYC

    def x_peer(d):
        return (x + d) % NX

    has_low = me > 0
    has_high = me < NBOX_DEV - 1

    barrier = pltpu.get_barrier_semaphore()
    offsets = peer_offsets()

    def signal(sem, box, level):
        pl.semaphore_signal(sem, inc=1, device_id=(box, level), device_id_type=mesh_ids)

    near_z = [d % NZ for k in range(RADIUS, 0, -1) for d in (k, -k)]
    for d in (2, 1, 3):
        signal(barrier, me, x_peer(d))
    for d in near_z:
        signal(barrier, z_peer(d), x)
    for d in range(1, NYC):
        signal(barrier, p_peer(d), x)

    loads = [
        pltpu.make_async_copy(src, dst, load_sem.at[i])
        for i, (src, dst) in enumerate((
            (cls_hbm, cls_ref), (rows_hbm, rows_ref), (rhs_hbm, rhs_ref), (expand_hbm, efull),
            (self_hbm, self_ref), (slot_hbm, slot_ref), (class_hbm, class_ref),
            (near_src_hbm, near_src_ref), (near_hbm, nops),
        ))
    ]
    for load in loads:
        load.start()
    loads[0].wait()

    eye2 = jnp.where(iota((64, 128), 0) == iota((64, 128), 1) % 64, 1.0, 0.0).astype(BF16)
    turned = lax.dot_general(
        cls_ref[...], eye2, (((0,), (0,)), ((), ())), preferred_element_type=F32
    ).astype(BF16)
    tout[...] = turned.reshape(NX, 64, 128)
    tin[x] = tout[x]

    pl.semaphore_wait(barrier, NX - 1 + len(near_z) + NYC - 1)
    for d in (2, 1, 3):
        start(tout.at[x_peer(d)], tin.at[x], t_send.at[d], t_recv.at[x], me, x_peer(d))

    for d in near_z:
        signal(known.at[0], z_peer(d), x)

    def know_two():
        pl.semaphore_wait(known.at[0], len(near_z))
        for d in (RADIUS, NZ - RADIUS):
            signal(known.at[1], z_peer(d), x)

    def know_three():
        pl.semaphore_wait(known.at[1], 2)
        for d in (NZ // 2 - 2 * RADIUS, NZ // 2 + 2 * RADIUS):
            signal(known.at[2], z_peer(d), x)

    def know_all():
        pl.semaphore_wait(known.at[2], 2)

    loads[1].wait()
    for j in range(2):
        hot = jnp.where(iota((128, 128), 0) == rows_ref[j:j + 1, :], 1.0, 0.0)
        tab[pl.ds(j, 128, stride=2), :] = hot.T
    sendoh[...] = tab[0:256, :].astype(BF16)

    lane128 = iota((16, 128), 1)
    low16 = lane128 < 64
    row_t = iota((16, 128), 0)
    rows64 = iota((64, 256), 0) % 16

    def halo_fill(it, v):
        half = v.astype(BF16)
        for r in range(4):
            hbuf[it, 1, :, r * 128:(r + 1) * 128] = half[r * 16:(r + 1) * 16]
        return half

    def halo_sends(it):
        low = remote(hbuf.at[it, 1], hbuf.at[it, 2], h_send.at[it, 0], h_recv.at[it, 1], me - 1, x)
        high = remote(hbuf.at[it, 1], hbuf.at[it, 0], h_send.at[it, 1], h_recv.at[it, 0], me + 1, x)

        @pl.when(has_low)
        def _():
            low.start()

        @pl.when(has_high)
        def _():
            high.start()

        @pl.when(jnp.logical_not(has_low))
        def _():
            hbuf[it, 0] = jnp.zeros((16, 512), BF16)

        @pl.when(jnp.logical_not(has_high))
        def _():
            hbuf[it, 2] = jnp.zeros((16, 512), BF16)

        return low, high

    def halo_settle(low, high):
        @pl.when(has_low)
        def _():
            low.wait_send()

        @pl.when(has_high)
        def _():
            high.wait_send()

    def multipoles(it, half):
        band = efull[:, pl.ds(pl.multiple_of(x * 64, 64), 64), :].reshape(1024, 128)
        full = dot_nt(half, band)
        doubled = []
        for r in range(4):
            total = jnp.zeros((16, 128), F32)
            for j in range(8):
                piece = full[r * 16:(r + 1) * 16, j * 128:(j + 1) * 128]
                total = total + jnp.where(
                    row_t == 2 * j + jnp.where(low16, 0, 1), piece, 0.0
                )
            doubled.append(total + pltpu.roll(total, 64, 1))
        for h in range(2):
            rows = jnp.where(low16, doubled[2 * h], doubled[2 * h + 1]).astype(BF16)
            picked = dot(sendoh[:, 0:16], rows)
            obuf[it, h] = picked.astype(BF16).reshape(NBOX_DEV, 2, 128)

    def multipole_sends(it, least=0, most=NZ):
        for offset in offsets:
            if not least <= min(offset[0], NZ - offset[0]) <= most:
                continue
            to = box_at(offset)
            remote(obuf.at[it, :, to], rbuf.at[it, :, me], a_send.at[it], a_recv.at[it],
                   to, x).start()
        if least == 0:
            rbuf[it, :, me] = obuf[it, :, me]

    def many(it):
        return rbuf.at[it, :, pl.ds(0, NBOX_DEV - 1)]

    def near_field(it, low, high):
        @pl.when(has_low)
        def _():
            high.wait_recv()

        @pl.when(has_high)
        def _():
            low.wait_recv()

        nbuf[...] = dot(nearoh[...], hbuf[it].reshape(48, 512)).astype(BF16)

        def one(c, acc):
            rows = nbuf[pl.ds(pl.multiple_of(c * 16, 16), 16), :]
            lhs = jnp.concatenate([rows[:, r * 128:(r + 1) * 128] for r in range(4)], axis=0)
            return acc + dot_nt(lhs, nops[c])

        return lax.fori_loop(0, 26, one, jnp.zeros((64, 128), F32), unroll=2)

    def pick_sources(it):
        arrived(many(it), a_recv.at[it])
        low = iota((256, 128), 1) < 64
        for h in range(2):
            a = rbuf[it, h].reshape(256, 128).astype(F32)
            b = pltpu.roll(a, 64, 1)
            for r, first, second in ((2 * h, a, b), (2 * h + 1, b, a)):
                lanes = slice(r * 128, (r + 1) * 128)
                r2[0:256, lanes] = jnp.where(low, first, 0.0).astype(BF16)
                r2[256:512, lanes] = jnp.where(low, 0.0, second).astype(BF16)

        for i in range(4):
            picked = dot(oh[i * 256:(i + 1) * 256, :], r2[...]).astype(BF16)
            for k in range(16):
                for r in range(4):
                    g2[r * 16:(r + 1) * 16, (i * 16 + k) * 128:(i * 16 + k + 1) * 128] = (
                        picked[k * 16:(k + 1) * 16, r * 128:(r + 1) * 128]
                    )

    def planes_product(group, part):
        arrived(wbuf.at[pl.ds(0, len(group) * NY)], sib_recv.at[part])
        total = jnp.zeros((64, 256), F32)
        for m in group:
            plane = (z - m + NZ) % NZ
            rows = g2[:, pl.ds(pl.multiple_of(plane * 512, 512), 512)]
            total = total + dot(rows, wbuf[pl.ds(plane * NYC, NYC)].reshape(512, 256))
        return total

    def local_far_sends(it, local):
        far = jnp.zeros((64, 128), F32)
        for t in range(16):
            far = far + dot(jnp.where(rows64 == t, local, 0.0).astype(BF16), efull[t])
        xbuf[it, x] = far.astype(BF16)
        for d in (2, 1, 3):
            start(xbuf.at[it, x], xbuf.at[it, x], x_send.at[it, d], x_recv.at[it, x],
                  me, x_peer(d))

    def far_sum(it):
        for d in range(1, NX):
            arrived(xbuf.at[it, x_peer(d)], x_recv.at[it, x_peer(d)])
        total = xbuf[it, 0].astype(F32)
        for k in range(1, NX):
            total = total + xbuf[it, k].astype(F32)
        return total

    lane1 = iota((1, 128), 1)

    def packed(pairs):
        rows = []
        for a, b in pairs:
            product = a * b
            for r in range(4):
                rows.append(jnp.sum(product[r * 16:(r + 1) * 16], axis=0, keepdims=True))
        stacked = jnp.concatenate(rows, axis=0)
        sums = jnp.sum(stacked, axis=1, keepdims=True)
        shape = (len(rows), 128)
        return jnp.sum(
            jnp.where(iota(shape, 0) == iota(shape, 1), sums, 0.0), axis=0, keepdims=True
        )

    def reduce_z(row):
        rz_out[...] = row
        for d in range(1, NZ):
            start(rz_out, rz.at[z], rz_send.at[d], rz_recv.at[z], z_peer(d), x)
        rz[z] = row

    def reduce_p():
        for d in range(1, NZ):
            src = (z + d) % NZ
            arrived(rz.at[src], rz_recv.at[src])
        row = jnp.sum(rz[...], axis=0)
        ry_out[...] = row
        for d in range(1, NYC):
            start(ry_out, ry.at[yc], ry_send.at[d], ry_recv.at[yc], p_peer(d), x)
        ry[yc] = row

    def reduced():
        for d in range(1, NYC):
            src = (yc + d) % NYC
            arrived(ry.at[src], ry_recv.at[src])
        return jnp.sum(ry[...], axis=0)

    def reduce_all(row):
        ra_out[...] = row
        for offset in offsets:
            remote(ra_out, rall.at[me], ra_send, ra_recv, box_at(offset), x).start()
        rall[me] = row
        arrived(rall.at[pl.ds(0, NBOX_DEV - 1)], ra_recv)
        return jnp.sum(rall[...], axis=0)

    def spread(row):
        return jnp.concatenate(
            [
                jnp.broadcast_to(
                    jnp.sum(jnp.where(lane1 == r, row, 0.0), axis=1, keepdims=True), (16, 128)
                )
                for r in range(4)
            ],
            axis=0,
        )

    loads[2].wait()
    loads[4].wait()
    v = rhs_ref[...].reshape(64, 128)
    diag = jnp.concatenate([self_ref[...]] * 4, axis=0)
    half = halo_fill(0, v)
    loads[3].wait()
    multipoles(0, half)

    for d in range(1, NX):
        arrived(tin.at[x_peer(d)], t_recv.at[x_peer(d)])
    low_t = iota((64, 128), 1) < 64
    merged = [
        jnp.where(low_t, tin[2 * h].astype(F32), tin[2 * h + 1].astype(F32)) for h in range(2)
    ]
    wbuf[me] = jnp.concatenate(merged, axis=1).astype(BF16)

    def cls_at(m, y_rel):
        return wbuf.at[((z - m + NZ) % NZ) * NYC + ((y + y_rel) % NY) * NC + core]

    def relay(m, reach):
        ref = cls_at(m, 0)
        ways = ((0, 1), (1, -1)) if m == 0 else (((0, 1),) if m <= NZ // 2 else ((1, -1),))
        gone = m if m <= NZ // 2 else NZ - m
        for d in range(HOP, 0, -1):
            for way, sign in ways:
                at = gone + d
                if at <= reach[way]:
                    start(ref, ref, ring_send.at[way, at], ring_recv.at[way, at],
                          z_peer(sign * d % NZ), x)

    reach = (NZ // 2, NZ // 2 - 1)

    def y_out(m):
        ref = cls_at(m, 0)
        up = z * NYC + ((y + 1) % NY) * NC + core
        down = z * NYC + ((y + 3) % NY) * NC + core
        start(ref, ref, y_send.at[0, m], y_recv.at[0, m], up, x)
        start(ref, ref, y_send.at[1, m], y_recv.at[1, m], down, x)
        if m in FAR_DIRECT:
            across = z * NYC + ((y + 2) % NY) * NC + core
            start(ref, ref, y_send.at[2, m], y_recv.at[2, m], across, x)

    def sibling(m, y_rel):
        ref = cls_at(m, y_rel)
        start(ref, ref, sib_send.at[y_rel, m], sib_recv.at[0 if m in EARLY else 1],
              z * NYC + y * NC + 1 - core, x)

    def z_in(m):
        gone = m if m <= NZ // 2 else NZ - m
        way = 0 if m <= NZ // 2 else 1
        arrived(cls_at(m, 0), ring_recv.at[way, gone])
        if gone % HOP == 0:
            relay(m, reach)
        y_out(m)
        sibling(m, 0)

    def y_in(m):
        arrived(cls_at(m, 3), y_recv.at[0, m])
        arrived(cls_at(m, 1), y_recv.at[1, m])
        if m not in FAR_DIRECT:
            if m % 2 == 0:
                ref = cls_at(m, 3)
                to = z * NYC + ((y + 1) % NY) * NC + core
            else:
                ref = cls_at(m, 1)
                to = z * NYC + ((y + 3) % NY) * NC + core
            start(ref, ref, y_send.at[2, m], y_recv.at[2, m], to, x)
        sibling(m, 3)
        sibling(m, 1)

    def y_far_in(m):
        arrived(cls_at(m, 2), y_recv.at[2, m])
        sibling(m, 2)

    relay(0, reach)
    y_out(0)
    sibling(0, 0)

    iota_c = iota((128, 64), 0)
    for load in loads[5:8]:
        load.wait()
    for t in range(16):
        match = iota_c == class_ref[t:t + 1, :]
        value = jnp.where(match, (slot_ref[t:t + 1, :] + 1).astype(F32), 0.0)
        tab[pl.ds(t, 128, stride=16), :] = jnp.broadcast_to(
            jnp.sum(value, axis=1, keepdims=True), (128, 128)
        )

    def hot_rows(i, carry):
        at = pl.multiple_of(i * 32, 32)
        for k in range(2):
            want = tab[pl.ds(at + k * 16, 16), :]
            for part in range(2):
                slots = (lane128 + (part * 128 + 1)).astype(F32)
                oh[pl.ds(pl.multiple_of(i * 16, 16), 16),
                   k * 256 + part * 128:k * 256 + (part + 1) * 128] = jnp.where(
                       want == slots, 1.0, 0.0).astype(BF16)
        return carry

    lax.fori_loop(0, 64, hot_rows, 0, unroll=4)
    know_two()
    low_copy, high_copy = halo_sends(0)
    multipole_sends(0, 0, 3)
    for m in (2, 14, 1, 15):
        z_in(m)
    y_in(0)
    know_three()
    multipole_sends(0, 4, 6)
    for c in range(26):
        nearoh[c * 16:(c + 1) * 16, :] = jnp.where(
            near_src_ref[:, c:c + 1] == iota((16, 48), 1), 1.0, 0.0
        ).astype(BF16)

    loads[8].wait()
    for m in (4, 12, 3, 13):
        z_in(m)
    for m in (2, 14, 1, 15):
        y_in(m)
    know_all()
    multipole_sends(0, 7, 8)
    near_one = near_field(0, low_copy, high_copy)
    for m in (6, 10, 5, 11):
        z_in(m)
    y_far_in(0)
    for m in (4, 12, 3, 13):
        y_in(m)
    for m in (8, 7, 9):
        z_in(m)
    for m in (2, 14, 1, 15):
        y_far_in(m)
    for m in (6, 10, 5, 11):
        y_in(m)
    pick_sources(0)
    for m in (4, 12, 3, 13):
        y_far_in(m)
    for m in (8, 7, 9):
        y_in(m)
    local_one = planes_product(EARLY, 0)
    for m in (6, 10, 5, 11, 8, 7, 9):
        y_far_in(m)
    local_one = local_one + planes_product(LATE, 1)

    local_far_sends(0, local_one)
    base = diag * v + near_one
    image = base + far_sum(0)

    shifted = image - SHIFT * v
    half = halo_fill(1, shifted)
    multipoles(1, half)
    multipole_sends(1)
    low_two, high_two = halo_sends(1)
    reduce_z(packed([(v, v), (v, image)]))
    near_two = near_field(1, low_two, high_two)
    sent(many(0), a_send.at[0])
    halo_settle(low_copy, high_copy)
    reduce_p()
    pick_sources(1)
    local_far_sends(1, dot(g2[...], wbuf[...].reshape(8192, 256)))

    rr = reduced()
    ra = pltpu.roll(rr, 124, 1)
    h11 = ra / rr
    slope = spread(h11)
    u = image - slope * v
    base = diag * shifted + near_two - (slope - SHIFT) * image
    settle()
    halo_settle(low_two, high_two)
    sent(many(1), a_send.at[1])
    b = base + far_sum(1)
    uu = reduce_all(packed([(u, u), (v, b), (u, b), (b, b)]))
    rb = pltpu.roll(uu, 124, 1)
    ub = pltpu.roll(uu, 120, 1)
    bb = pltpu.roll(uu, 116, 1)
    beta = jnp.sqrt(rr)
    length = jnp.sqrt(uu)
    h21 = length / beta
    h12 = rb / (beta * length)
    h22 = ub / uu
    gram_aa = h11 * h11 + h21 * h21
    gram_ab = h11 * h12 + h21 * h22
    gram_bb = bb / uu
    right_a = beta * h11
    right_b = beta * h12
    det = gram_aa * gram_bb - gram_ab * gram_ab
    coef_a = (gram_bb * right_a - gram_ab * right_b) / det / beta
    coef_b = (gram_aa * right_b - gram_ab * right_a) / det / length
    out_ref[...] = (spread(coef_a) * v + spread(coef_b) * u).reshape(4, 16, 128)
    sent(rall.at[pl.ds(0, NBOX_DEV - 1)], ra_send)


def per_device(
    rhs_field, self_coef, expand, near_ops, class_ops, near_src, send_rows, list_slot, list_class
):
    vmem = pl.BlockSpec(memory_space=pltpu.VMEM)
    hbm = pl.BlockSpec(memory_space=pltpu.HBM)
    dma = pltpu.SemaphoreType.DMA
    return pl.pallas_call(
        body,
        out_shape=jax.ShapeDtypeStruct((4, 16, 128), F32),
        in_specs=[hbm] * 9,
        out_specs=vmem,
        scratch_shapes=[
            pltpu.VMEM((4, 16, 128), F32),
            pltpu.VMEM((16, 128), F32),
            pltpu.VMEM((64, 256), BF16),
            pltpu.VMEM((16, 26), jnp.int32),
            pltpu.VMEM((2, 128), jnp.int32),
            pltpu.VMEM((16, 64), jnp.int32),
            pltpu.VMEM((16, 64), jnp.int32),
            pltpu.VMEM((16, 256, 128), BF16),
            pltpu.VMEM((26, 128, 128), BF16),
            pltpu.VMEM((NX, 64, 128), BF16),
            pltpu.VMEM((NX, 64, 128), BF16),
            pltpu.VMEM((NBOX_DEV, 64, 256), BF16),
            pltpu.VMEM((2, 3, 16, 512), BF16),
            pltpu.VMEM((2, 2, NBOX_DEV, 2, 128), BF16),
            pltpu.VMEM((2, 2, NBOX_DEV, 2, 128), BF16),
            pltpu.VMEM((512, 512), BF16),
            pltpu.VMEM((64, 8192), BF16),
            pltpu.VMEM((416, 512), BF16),
            pltpu.VMEM((2, NX, 64, 128), BF16),
            pltpu.VMEM((2048, 128), F32),
            pltpu.VMEM((1024, 512), BF16),
            pltpu.VMEM((416, 48), BF16),
            pltpu.VMEM((256, 128), BF16),
            pltpu.VMEM((1, 128), F32),
            pltpu.VMEM((NZ, 1, 128), F32),
            pltpu.VMEM((1, 128), F32),
            pltpu.VMEM((NYC, 1, 128), F32),
            pltpu.VMEM((1, 128), F32),
            pltpu.VMEM((NBOX_DEV, 1, 128), F32),
            dma((9,)),
            dma((NX,)), dma((NX,)),
            dma((2, 9)), dma((2, 9)),
            dma((3, NZ)), dma((3, NZ)),
            dma((NY, NZ)), dma((2,)),
            dma((2, 2)), dma((2, 2)),
            dma((2,)), dma((2,)),
            dma((2, NX)), dma((2, NX)),
            dma((NZ,)), dma((NZ,)),
            dma((NYC,)), dma((NYC,)),
            dma, dma,
            pltpu.SemaphoreType.REGULAR((3,)),
        ],
        compiler_params=pltpu.CompilerParams(
            collective_id=0, has_side_effects=True, vmem_limit_bytes=62 * 1024 * 1024
        ),
        cost_estimate=pl.CostEstimate(
            flops=4_000_000_000, bytes_accessed=4_000_000, transcendentals=0
        ),
    )(
        rhs_field, self_coef, expand, near_ops, class_ops[0], near_src, send_rows[0].T,
        list_slot, list_class,
    )


def solution(mesh):
    return jax.shard_map(
        per_device,
        mesh=mesh,
        in_specs=(
            P(None, "box", None),
            P("box", None),
            P("box", None, None),
            P(),
            P("box", "level", None),
            P("box", None),
            P("box", None, None),
            P("box", None),
            P("box", None),
        ),
        out_specs=P(None, "box", None),
        check_vma=False,
    )
```

```python
import jax
import jax.numpy as jnp
from jax import lax
from jax.experimental import pallas as pl
from jax.experimental.pallas import tpu as pltpu
from jax.sharding import PartitionSpec as P

NZ, NY, NC, NX = 16, 4, 2, 4
NYC = NY * NC
SHIFT = 3.0
RADIUS = 3
HOP = 2
FAR_DIRECT = (7, 8, 9)
EARLY = (0, 1, 15, 2, 14, 3, 13, 4, 12)
LATE = (5, 11, 6, 10, 7, 9, 8)
NBOX_DEV = NZ * NYC
F32, BF16 = jnp.float32, jnp.bfloat16


def dot(a, b):
    return jnp.dot(a, b, preferred_element_type=F32)


def dot_nt(a, b):
    return lax.dot_general(a, b, (((1,), (1,)), ((), ())), preferred_element_type=F32)


def iota(shape, dim):
    return lax.broadcasted_iota(jnp.int32, shape, dim)


def peer_offsets():
    offsets = [
        (dz, dy, dc) for dz in range(NZ) for dy in range(NY) for dc in range(NC)
        if (dz, dy, dc) != (0, 0, 0)
    ]
    return sorted(offsets, key=lambda o: -(2 * min(o[0], NZ - o[0]) + 2 * min(o[1], NY - o[1]) + o[2]))


def body(
    rhs_hbm, self_hbm, expand_hbm, near_hbm, cls_hbm, near_src_hbm, rows_hbm, slot_hbm, class_hbm,
    out_ref,
    rhs_ref, self_ref, cls_ref, near_src_ref, rows_ref, slot_ref, class_ref,
    efull, nops, tout, tin, wbuf, hbuf, obuf, rbuf, r2, g2, nbuf, xbuf, tab, oh, nearoh, sendoh,
    rz_out, rz, ry_out, ry, ra_out, rall,
    load_sem, t_send, t_recv, ring_send, ring_recv, y_send, y_recv, sib_send, sib_recv,
    h_send, h_recv, a_send, a_recv, x_send, x_recv,
    rz_send, rz_recv, ry_send, ry_recv, ra_send, ra_recv, known,
):
    me = lax.axis_index("box")
    x = lax.axis_index("level")
    z = me // NYC
    yc = me % NYC
    y = yc // NC
    core = yc % NC
    sends = []
    mesh_ids = pl.DeviceIdType.MESH

    def remote(src, dst, ssem, rsem, box, level):
        return pltpu.make_async_remote_copy(
            src_ref=src, dst_ref=dst, send_sem=ssem, recv_sem=rsem,
            device_id=(box, level), device_id_type=mesh_ids,
        )

    def start(src, dst, ssem, rsem, box, level):
        copy = remote(src, dst, ssem, rsem, box, level)
        copy.start()
        sends.append(copy)

    blocks = {"ring": 0, "y": 0, "sib": 0}

    def pass_on(kind, ref, ssem, rsem, box):
        remote(ref, ref, ssem, rsem, box, x).start()
        blocks[kind] += 1

    def arrived(dst, rsem):
        remote(dst, dst, rsem, rsem, me, x).wait_recv()

    def sent(ref, ssem):
        remote(ref, ref, ssem, ssem, me, x).wait_send()

    def settle():
        for copy in sends:
            copy.wait_send()
        sends.clear()

    def box_at(offset):
        dz, dy, dc = offset
        return ((z + dz) % NZ) * NYC + ((y + dy) % NY) * NC + (core + dc) % NC

    def z_peer(d):
        return ((z + d) % NZ) * NYC + yc

    def p_peer(d):
        return z * NYC + (yc + d) % NYC

    def x_peer(d):
        return (x + d) % NX

    has_low = me > 0
    has_high = me < NBOX_DEV - 1

    barrier = pltpu.get_barrier_semaphore()
    offsets = peer_offsets()

    def signal(sem, box, level):
        pl.semaphore_signal(sem, inc=1, device_id=(box, level), device_id_type=mesh_ids)

    near_z = [d % NZ for k in range(RADIUS, 0, -1) for d in (k, -k)]
    for d in (2, 1, 3):
        signal(barrier, me, x_peer(d))
    for d in near_z:
        signal(barrier, z_peer(d), x)
    for d in range(1, NYC):
        signal(barrier, p_peer(d), x)

    loads = [
        pltpu.make_async_copy(src, dst, load_sem.at[i])
        for i, (src, dst) in enumerate((
            (cls_hbm, cls_ref), (rows_hbm, rows_ref), (rhs_hbm, rhs_ref), (expand_hbm, efull),
            (self_hbm, self_ref), (slot_hbm, slot_ref), (class_hbm, class_ref),
            (near_src_hbm, near_src_ref), (near_hbm, nops),
        ))
    ]
    for load in loads:
        load.start()
    loads[0].wait()

    eye2 = jnp.where(iota((64, 128), 0) == iota((64, 128), 1) % 64, 1.0, 0.0).astype(BF16)
    turned = lax.dot_general(
        cls_ref[...], eye2, (((0,), (0,)), ((), ())), preferred_element_type=F32
    ).astype(BF16)
    tout[...] = turned.reshape(NX, 64, 128)
    tin[x] = tout[x]

    pl.semaphore_wait(barrier, NX - 1 + len(near_z) + NYC - 1)
    for d in (2, 1, 3):
        start(tout.at[x_peer(d)], tin.at[x], t_send.at[d], t_recv.at[x], me, x_peer(d))

    for d in near_z:
        signal(known.at[0], z_peer(d), x)

    def know_two():
        pl.semaphore_wait(known.at[0], len(near_z))
        for d in (RADIUS, NZ - RADIUS):
            signal(known.at[1], z_peer(d), x)

    def know_three():
        pl.semaphore_wait(known.at[1], 2)
        for d in (NZ // 2 - 2 * RADIUS, NZ // 2 + 2 * RADIUS):
            signal(known.at[2], z_peer(d), x)

    def know_all():
        pl.semaphore_wait(known.at[2], 2)

    loads[1].wait()
    for j in range(2):
        hot = jnp.where(iota((128, 128), 0) == rows_ref[j:j + 1, :], 1.0, 0.0)
        tab[pl.ds(j, 128, stride=2), :] = hot.T
    sendoh[...] = tab[0:256, :].astype(BF16)

    lane128 = iota((16, 128), 1)
    low16 = lane128 < 64
    row_t = iota((16, 128), 0)
    rows64 = iota((64, 256), 0) % 16

    def halo_fill(it, v):
        half = v.astype(BF16)
        for r in range(4):
            hbuf[it, 1, :, r * 128:(r + 1) * 128] = half[r * 16:(r + 1) * 16]
        return half

    def halo_sends(it):
        low = remote(hbuf.at[it, 1], hbuf.at[it, 2], h_send.at[it, 0], h_recv.at[it, 1], me - 1, x)
        high = remote(hbuf.at[it, 1], hbuf.at[it, 0], h_send.at[it, 1], h_recv.at[it, 0], me + 1, x)

        @pl.when(has_low)
        def _():
            low.start()

        @pl.when(has_high)
        def _():
            high.start()

        @pl.when(jnp.logical_not(has_low))
        def _():
            hbuf[it, 0] = jnp.zeros((16, 512), BF16)

        @pl.when(jnp.logical_not(has_high))
        def _():
            hbuf[it, 2] = jnp.zeros((16, 512), BF16)

        return low, high

    def halo_settle(low, high):
        @pl.when(has_low)
        def _():
            low.wait_send()

        @pl.when(has_high)
        def _():
            high.wait_send()

    def multipoles(it, half):
        band = efull[:, pl.ds(pl.multiple_of(x * 64, 64), 64), :].reshape(1024, 128)
        full = dot_nt(half, band)
        doubled = []
        for r in range(4):
            total = jnp.zeros((16, 128), F32)
            for j in range(8):
                piece = full[r * 16:(r + 1) * 16, j * 128:(j + 1) * 128]
                total = total + jnp.where(
                    row_t == 2 * j + jnp.where(low16, 0, 1), piece, 0.0
                )
            doubled.append(total + pltpu.roll(total, 64, 1))
        for h in range(2):
            rows = jnp.where(low16, doubled[2 * h], doubled[2 * h + 1]).astype(BF16)
            picked = dot(sendoh[:, 0:16], rows)
            obuf[it, h] = picked.astype(BF16).reshape(NBOX_DEV, 2, 128)

    def multipole_sends(it, least=0, most=NZ):
        for offset in offsets:
            if not least <= min(offset[0], NZ - offset[0]) <= most:
                continue
            to = box_at(offset)
            remote(obuf.at[it, :, to], rbuf.at[it, :, me], a_send.at[it], a_recv.at[it],
                   to, x).start()
        if least == 0:
            rbuf[it, :, me] = obuf[it, :, me]

    def many(it):
        return rbuf.at[it, :, pl.ds(0, NBOX_DEV - 1)]

    def near_field(it, low, high):
        @pl.when(has_low)
        def _():
            high.wait_recv()

        @pl.when(has_high)
        def _():
            low.wait_recv()

        nbuf[...] = dot(nearoh[...], hbuf[it].reshape(48, 512)).astype(BF16)

        def one(c, acc):
            rows = nbuf[pl.ds(pl.multiple_of(c * 16, 16), 16), :]
            lhs = jnp.concatenate([rows[:, r * 128:(r + 1) * 128] for r in range(4)], axis=0)
            return acc + dot_nt(lhs, nops[c])

        return lax.fori_loop(0, 26, one, jnp.zeros((64, 128), F32), unroll=2)

    def pick_sources(it):
        arrived(many(it), a_recv.at[it])
        low = iota((256, 128), 1) < 64
        for h in range(2):
            a = rbuf[it, h].reshape(256, 128).astype(F32)
            b = pltpu.roll(a, 64, 1)
            for r, first, second in ((2 * h, a, b), (2 * h + 1, b, a)):
                lanes = slice(r * 128, (r + 1) * 128)
                r2[0:256, lanes] = jnp.where(low, first, 0.0).astype(BF16)
                r2[256:512, lanes] = jnp.where(low, 0.0, second).astype(BF16)

        for i in range(4):
            picked = dot(oh[i * 256:(i + 1) * 256, :], r2[...]).astype(BF16)
            for k in range(16):
                for r in range(4):
                    g2[r * 16:(r + 1) * 16, (i * 16 + k) * 128:(i * 16 + k + 1) * 128] = (
                        picked[k * 16:(k + 1) * 16, r * 128:(r + 1) * 128]
                    )

    def planes_product(group, part):
        arrived(wbuf.at[pl.ds(0, len(group) * NY)], sib_recv.at[part])
        total = jnp.zeros((64, 256), F32)
        for m in group:
            plane = (z - m + NZ) % NZ
            rows = g2[:, pl.ds(pl.multiple_of(plane * 512, 512), 512)]
            total = total + dot(rows, wbuf[pl.ds(plane * NYC, NYC)].reshape(512, 256))
        return total

    def local_far_sends(it, local):
        far = jnp.zeros((64, 128), F32)
        for t in range(16):
            far = far + dot(jnp.where(rows64 == t, local, 0.0).astype(BF16), efull[t])
        xbuf[it, x] = far.astype(BF16)
        for d in (2, 1, 3):
            start(xbuf.at[it, x], xbuf.at[it, x], x_send.at[it, d], x_recv.at[it, x],
                  me, x_peer(d))

    def far_sum(it):
        for d in range(1, NX):
            arrived(xbuf.at[it, x_peer(d)], x_recv.at[it, x_peer(d)])
        total = xbuf[it, 0].astype(F32)
        for k in range(1, NX):
            total = total + xbuf[it, k].astype(F32)
        return total

    lane1 = iota((1, 128), 1)

    def packed(pairs):
        rows = []
        for a, b in pairs:
            product = a * b
            for r in range(4):
                rows.append(jnp.sum(product[r * 16:(r + 1) * 16], axis=0, keepdims=True))
        stacked = jnp.concatenate(rows, axis=0)
        sums = jnp.sum(stacked, axis=1, keepdims=True)
        shape = (len(rows), 128)
        return jnp.sum(
            jnp.where(iota(shape, 0) == iota(shape, 1), sums, 0.0), axis=0, keepdims=True
        )

    def reduce_z(row):
        rz_out[...] = row
        for d in range(1, NZ):
            remote(rz_out, rz.at[z], rz_send, rz_recv, z_peer(d), x).start()
        rz[z] = row

    def reduce_p():
        arrived(rz.at[pl.ds(0, NZ - 1)], rz_recv)
        row = jnp.sum(rz[...], axis=0)
        ry_out[...] = row
        for d in range(1, NYC):
            remote(ry_out, ry.at[yc], ry_send, ry_recv, p_peer(d), x).start()
        ry[yc] = row

    def reduced():
        arrived(ry.at[pl.ds(0, NYC - 1)], ry_recv)
        return jnp.sum(ry[...], axis=0)

    def reduce_all(row):
        ra_out[...] = row
        for offset in offsets:
            remote(ra_out, rall.at[me], ra_send, ra_recv, box_at(offset), x).start()
        rall[me] = row
        arrived(rall.at[pl.ds(0, NBOX_DEV - 1)], ra_recv)
        return jnp.sum(rall[...], axis=0)

    def spread(row):
        return jnp.concatenate(
            [
                jnp.broadcast_to(
                    jnp.sum(jnp.where(lane1 == r, row, 0.0), axis=1, keepdims=True), (16, 128)
                )
                for r in range(4)
            ],
            axis=0,
        )

    loads[2].wait()
    loads[4].wait()
    v = rhs_ref[...].reshape(64, 128)
    diag = jnp.concatenate([self_ref[...]] * 4, axis=0)
    half = halo_fill(0, v)
    loads[3].wait()
    multipoles(0, half)

    for d in range(1, NX):
        arrived(tin.at[x_peer(d)], t_recv.at[x_peer(d)])
    low_t = iota((64, 128), 1) < 64
    merged = [
        jnp.where(low_t, tin[2 * h].astype(F32), tin[2 * h + 1].astype(F32)) for h in range(2)
    ]
    wbuf[me] = jnp.concatenate(merged, axis=1).astype(BF16)

    def cls_at(m, y_rel):
        return wbuf.at[((z - m + NZ) % NZ) * NYC + ((y + y_rel) % NY) * NC + core]

    def relay(m, reach):
        ref = cls_at(m, 0)
        ways = ((0, 1), (1, -1)) if m == 0 else (((0, 1),) if m <= NZ // 2 else ((1, -1),))
        gone = m if m <= NZ // 2 else NZ - m
        for d in range(HOP, 0, -1):
            for way, sign in ways:
                at = gone + d
                if at <= reach[way]:
                    pass_on("ring", ref, ring_send, ring_recv.at[way, at],
                            z_peer(sign * d % NZ))

    reach = (NZ // 2, NZ // 2 - 1)

    def y_out(m):
        ref = cls_at(m, 0)
        up = z * NYC + ((y + 1) % NY) * NC + core
        down = z * NYC + ((y + 3) % NY) * NC + core
        pass_on("y", ref, y_send, y_recv.at[0, m], up)
        pass_on("y", ref, y_send, y_recv.at[1, m], down)
        if m in FAR_DIRECT:
            across = z * NYC + ((y + 2) % NY) * NC + core
            pass_on("y", ref, y_send, y_recv.at[2, m], across)

    def sibling(m, y_rel):
        ref = cls_at(m, y_rel)
        pass_on("sib", ref, sib_send, sib_recv.at[0 if m in EARLY else 1],
                z * NYC + y * NC + 1 - core)

    def z_in(m):
        gone = m if m <= NZ // 2 else NZ - m
        way = 0 if m <= NZ // 2 else 1
        arrived(cls_at(m, 0), ring_recv.at[way, gone])
        if gone % HOP == 0:
            relay(m, reach)
        y_out(m)
        sibling(m, 0)

    def y_in(m):
        arrived(cls_at(m, 3), y_recv.at[0, m])
        arrived(cls_at(m, 1), y_recv.at[1, m])
        if m not in FAR_DIRECT:
            if m % 2 == 0:
                ref = cls_at(m, 3)
                to = z * NYC + ((y + 1) % NY) * NC + core
            else:
                ref = cls_at(m, 1)
                to = z * NYC + ((y + 3) % NY) * NC + core
            pass_on("y", ref, y_send, y_recv.at[2, m], to)
        sibling(m, 3)
        sibling(m, 1)

    def y_far_in(m):
        arrived(cls_at(m, 2), y_recv.at[2, m])
        sibling(m, 2)

    relay(0, reach)
    y_out(0)
    sibling(0, 0)

    iota_c = iota((128, 64), 0)
    for load in loads[5:8]:
        load.wait()
    for t in range(16):
        match = iota_c == class_ref[t:t + 1, :]
        value = jnp.where(match, (slot_ref[t:t + 1, :] + 1).astype(F32), 0.0)
        tab[pl.ds(t, 128, stride=16), :] = jnp.broadcast_to(
            jnp.sum(value, axis=1, keepdims=True), (128, 128)
        )

    def hot_rows(i, carry):
        at = pl.multiple_of(i * 32, 32)
        for k in range(2):
            want = tab[pl.ds(at + k * 16, 16), :]
            for part in range(2):
                slots = (lane128 + (part * 128 + 1)).astype(F32)
                oh[pl.ds(pl.multiple_of(i * 16, 16), 16),
                   k * 256 + part * 128:k * 256 + (part + 1) * 128] = jnp.where(
                       want == slots, 1.0, 0.0).astype(BF16)
        return carry

    lax.fori_loop(0, 64, hot_rows, 0, unroll=4)
    know_two()
    low_copy, high_copy = halo_sends(0)
    multipole_sends(0, 0, 3)
    for m in (2, 14, 1, 15):
        z_in(m)
    y_in(0)
    know_three()
    multipole_sends(0, 4, 6)
    for c in range(26):
        nearoh[c * 16:(c + 1) * 16, :] = jnp.where(
            near_src_ref[:, c:c + 1] == iota((16, 48), 1), 1.0, 0.0
        ).astype(BF16)

    loads[8].wait()
    for m in (4, 12, 3, 13):
        z_in(m)
    for m in (2, 14, 1, 15):
        y_in(m)
    know_all()
    multipole_sends(0, 7, 8)
    near_one = near_field(0, low_copy, high_copy)
    for m in (6, 10, 5, 11):
        z_in(m)
    y_far_in(0)
    for m in (4, 12, 3, 13):
        y_in(m)
    for m in (8, 7, 9):
        z_in(m)
    for m in (2, 14, 1, 15):
        y_far_in(m)
    for m in (6, 10, 5, 11):
        y_in(m)
    pick_sources(0)
    for m in (4, 12, 3, 13):
        y_far_in(m)
    for m in (8, 7, 9):
        y_in(m)
    local_one = planes_product(EARLY, 0)
    for m in (6, 10, 5, 11, 8, 7, 9):
        y_far_in(m)
    local_one = local_one + planes_product(LATE, 1)

    local_far_sends(0, local_one)
    base = diag * v + near_one
    image = base + far_sum(0)

    shifted = image - SHIFT * v
    half = halo_fill(1, shifted)
    low_two, high_two = halo_sends(1)
    multipoles(1, half)
    multipole_sends(1)
    reduce_z(packed([(v, v), (v, image)]))
    near_two = near_field(1, low_two, high_two)
    sent(many(0), a_send.at[0])
    halo_settle(low_copy, high_copy)
    for kind, ssem in (("ring", ring_send), ("y", y_send), ("sib", sib_send)):
        sent(wbuf.at[pl.ds(0, blocks[kind])], ssem)
    settle()
    pick_sources(1)
    reduce_p()
    local_far_sends(1, dot(g2[...], wbuf[...].reshape(8192, 256)))

    rr = reduced()
    ra = pltpu.roll(rr, 124, 1)
    h11 = ra / rr
    slope = spread(h11)
    u = image - slope * v
    base = diag * shifted + near_two - (slope - SHIFT) * image
    b = base + far_sum(1)
    uu = reduce_all(packed([(u, u), (v, b), (u, b), (b, b)]))
    rb = pltpu.roll(uu, 124, 1)
    ub = pltpu.roll(uu, 120, 1)
    bb = pltpu.roll(uu, 116, 1)
    beta = jnp.sqrt(rr)
    length = jnp.sqrt(uu)
    h21 = length / beta
    h12 = rb / (beta * length)
    h22 = ub / uu
    gram_aa = h11 * h11 + h21 * h21
    gram_ab = h11 * h12 + h21 * h22
    gram_bb = bb / uu
    right_a = beta * h11
    right_b = beta * h12
    det = gram_aa * gram_bb - gram_ab * gram_ab
    coef_a = (gram_bb * right_a - gram_ab * right_b) / det / beta
    coef_b = (gram_aa * right_b - gram_ab * right_a) / det / length
    out_ref[...] = (spread(coef_a) * v + spread(coef_b) * u).reshape(4, 16, 128)
    settle()
    halo_settle(low_two, high_two)
    sent(many(1), a_send.at[1])
    sent(rz.at[pl.ds(0, NZ - 1)], rz_send)
    sent(ry.at[pl.ds(0, NYC - 1)], ry_send)
    sent(rall.at[pl.ds(0, NBOX_DEV - 1)], ra_send)


def per_device(
    rhs_field, self_coef, expand, near_ops, class_ops, near_src, send_rows, list_slot, list_class
):
    vmem = pl.BlockSpec(memory_space=pltpu.VMEM)
    hbm = pl.BlockSpec(memory_space=pltpu.HBM)
    dma = pltpu.SemaphoreType.DMA
    return pl.pallas_call(
        body,
        out_shape=jax.ShapeDtypeStruct((4, 16, 128), F32),
        in_specs=[hbm] * 9,
        out_specs=vmem,
        scratch_shapes=[
            pltpu.VMEM((4, 16, 128), F32),
            pltpu.VMEM((16, 128), F32),
            pltpu.VMEM((64, 256), BF16),
            pltpu.VMEM((16, 26), jnp.int32),
            pltpu.VMEM((2, 128), jnp.int32),
            pltpu.VMEM((16, 64), jnp.int32),
            pltpu.VMEM((16, 64), jnp.int32),
            pltpu.VMEM((16, 256, 128), BF16),
            pltpu.VMEM((26, 128, 128), BF16),
            pltpu.VMEM((NX, 64, 128), BF16),
            pltpu.VMEM((NX, 64, 128), BF16),
            pltpu.VMEM((NBOX_DEV, 64, 256), BF16),
            pltpu.VMEM((2, 3, 16, 512), BF16),
            pltpu.VMEM((2, 2, NBOX_DEV, 2, 128), BF16),
            pltpu.VMEM((2, 2, NBOX_DEV, 2, 128), BF16),
            pltpu.VMEM((512, 512), BF16),
            pltpu.VMEM((64, 8192), BF16),
            pltpu.VMEM((416, 512), BF16),
            pltpu.VMEM((2, NX, 64, 128), BF16),
            pltpu.VMEM((2048, 128), F32),
            pltpu.VMEM((1024, 512), BF16),
            pltpu.VMEM((416, 48), BF16),
            pltpu.VMEM((256, 128), BF16),
            pltpu.VMEM((1, 128), F32),
            pltpu.VMEM((NZ, 1, 128), F32),
            pltpu.VMEM((1, 128), F32),
            pltpu.VMEM((NYC, 1, 128), F32),
            pltpu.VMEM((1, 128), F32),
            pltpu.VMEM((NBOX_DEV, 1, 128), F32),
            dma((9,)),
            dma((NX,)), dma((NX,)),
            dma, dma((2, 9)),
            dma, dma((3, NZ)),
            dma, dma((2,)),
            dma((2, 2)), dma((2, 2)),
            dma((2,)), dma((2,)),
            dma((2, NX)), dma((2, NX)),
            dma, dma,
            dma, dma,
            dma, dma,
            pltpu.SemaphoreType.REGULAR((3,)),
        ],
        compiler_params=pltpu.CompilerParams(
            collective_id=0, has_side_effects=True, vmem_limit_bytes=62 * 1024 * 1024
        ),
        cost_estimate=pl.CostEstimate(
            flops=4_000_000_000, bytes_accessed=4_000_000, transcendentals=0
        ),
    )(
        rhs_field, self_coef, expand, near_ops, class_ops[0], near_src, send_rows[0].T,
        list_slot, list_class,
    )


def solution(mesh):
    return jax.shard_map(
        per_device,
        mesh=mesh,
        in_specs=(
            P(None, "box", None),
            P("box", None),
            P("box", None, None),
            P(),
            P("box", "level", None),
            P("box", None),
            P("box", None, None),
            P("box", None),
            P("box", None),
        ),
        out_specs=P(None, "box", None),
        check_vma=False,
    )
```
